256 devices in a mesh: dom: 32 (over x, z), cls: 8 (over y, core).
Axes of the slice: x: 4, y: 4, z: 8, core: 2. Of those that a mesh axis runs over, the one named last changes fastest.
Arguments:
- particles: bfloat16 [256, 1024, 9, 128], P(None, ('dom', 'cls')), may hold values from -6 to 6
- references: bfloat16 [256, 400, 128], P(None, 'cls'), may hold values from -6 to 6
- class_ids: int32 [1024, 3], P(('dom', 'cls')), may hold values from 0 to 399, all different within a row
- counts: int32 [1024], P(('dom', 'cls')), may hold values from 1 to 3
- shift_ids: int32 [1024, 3], P(('dom', 'cls')), may hold values from 0 to 8
- weights: bfloat16 [1024, 3], P(('dom', 'cls')), may hold values from 0.049804688 to 1
Outputs:
- best_scores: float32 [1024, 400], P('dom', 'cls')
- class_means: float32 [256, 400, 128], P('dom', 'cls')
The draws below stay inside these ranges and needn't reach their ends.
Inputs may be any that keep to these rules, and one draw needn't show every extreme that they name: `class_ids`: each particle's row names 3 different classes and every class is named by some row; only the first counts entries of a row are significant.
All inputs are finite; a program needn't handle non-finite values.
Results may differ from the reference program's by a relative error of at most 0.0012.
Values may be sent and summed in bfloat16 or wider, within the bound.
No kernel may reach another device: no remote copies, remote signals or barrier semaphores. Data moves between devices by JAX's collectives and lax.ppermute only.
A program may use at most 128 MiB of HBM per device.

```python
import math
import jax
import jax.numpy as jnp
from jax import lax

CYCLES = 64
ANGLES = 256
SHIFTS = 9
SIGNIF = 3
CLASSES = 400
PARTICLES = 1024


def set_ends(entries, key, low, largest):
    shape = entries.shape
    spot = [jax.random.randint(jax.random.fold_in(key, axis), (), 0, shape[axis]) for axis in range(len(shape))]
    entries = entries.at[tuple(spot)].set(low)
    longest = shape.index(max(shape))
    spot[longest] = (spot[longest] + 1) % shape[longest]
    return entries.at[tuple(spot)].set(largest)


def level_of(own_key, extent, split, low, high):
    factor_of, own = 1.0, jax.random.fold_in(own_key, 6)
    for dim, parts in split:
        draws = jnp.exp(jax.random.uniform(jax.random.fold_in(own, dim), (parts,), jnp.float32, low / len(split), high / len(split)))
        factor_of = factor_of * jnp.repeat(draws, extent[dim] // parts).reshape([-1 if axis == dim else 1 for axis in range(len(extent))])
    return factor_of


def picks_of(rng, rows, number_of, top, lift):
    order = jax.random.permutation(jax.random.fold_in(rng, 1), number_of)
    favour = order
    for power in range(3):
        favour = favour * favour // number_of
    favour = favour * lift // number_of
    chance = jax.random.randint(jax.random.fold_in(rng, 2), (rows, number_of), 0, 4096) + favour
    fixed_rows = jax.random.permutation(jax.random.fold_in(rng, 3), rows)[jnp.arange(number_of) % rows]
    chance = jnp.where(jnp.arange(rows)[:, None] == fixed_rows[None, :], 1 << 14, chance)
    merit = chance * number_of + jnp.arange(number_of)
    return lax.top_k(merit.astype(jnp.int32), top)[1].astype(jnp.int32)


def noise(rng, shape, scale, most, split=(), kind=jnp.bfloat16):
    array = jax.random.normal(rng, shape, jnp.float32) * scale
    if len(split) > 0:
        array = level_of(rng, shape, split, -0.22, 0.18) * array
    return jnp.clip(array, min=-most, max=most).astype(kind)


def setup_inputs(seed: int = 0) -> dict:
    seeds = jax.random.split(jax.random.key(seed), 7)
    particles = noise(seeds[0], (ANGLES, PARTICLES, SHIFTS, 2 * CYCLES), 1.0, 6.0, ((1, 256),))
    references = noise(seeds[1], (ANGLES, CLASSES, 2 * CYCLES), 1.0, 6.0, ((1, 8),))
    class_ids = picks_of(seeds[2], PARTICLES, CLASSES, SIGNIF, 122)
    counts = set_ends(jax.random.randint(seeds[3], (PARTICLES,), 1, SIGNIF + 1), jax.random.fold_in(seeds[3], 1), 1, SIGNIF).astype(jnp.int32)
    shift_ids = set_ends(jax.random.randint(seeds[4], (PARTICLES, SIGNIF), 0, SHIFTS), jax.random.fold_in(seeds[4], 1), 0, SHIFTS - 1).astype(jnp.int32)
    weights = jnp.clip(jnp.exp(math.log(1.0) - 2.9996462 * jax.random.uniform(seeds[5], (PARTICLES, SIGNIF), jnp.float32) ** level_of(seeds[5], (PARTICLES, SIGNIF), ((0, 256),), -0.2, 0.2)), 0.049804688, 1.0).astype(jnp.bfloat16)
    return dict(particles=particles, references=references, class_ids=class_ids, counts=counts, shift_ids=shift_ids, weights=weights)


def angle_table(angles):
    harmonic = jnp.arange(angles, dtype=jnp.int32)
    product = harmonic[:, None] * harmonic[None, :] % angles
    phase_angle = product.astype(jnp.float32) * (2.0 * math.pi / angles)
    return jnp.stack([jnp.cos(phase_angle), -jnp.sin(phase_angle)]).astype(jnp.bfloat16)

def real_form(references, cycles):
    real_part = references[:, :, :cycles]
    imag_part = references[:, :, cycles:]
    swapped = jnp.concatenate([-imag_part, real_part], axis=2)
    return jnp.concatenate([references, swapped], axis=1)

def reference(particles, references, class_ids, counts, shift_ids, weights):
    table_wide = angle_table(ANGLES).astype(jnp.float32)
    stacked = real_form(references, CYCLES).astype(jnp.float32)
    scale = 1.0 / math.sqrt(2.0 * CYCLES * ANGLES)

    def score_one(image):
        products = jnp.einsum('msc,mqc->sqm', image.astype(jnp.float32), stacked)
        rounded = products.astype(jnp.bfloat16).astype(jnp.float32)
        rounded = rounded.reshape(SHIFTS, 2, CLASSES, ANGLES)
        scores = jnp.einsum('sekm,emp->skp', rounded, table_wide) * scale
        return lax.optimization_barrier(jnp.max(scores, axis=(0, 2)))
    best_scores = lax.map(score_one, jnp.transpose(particles, (1, 0, 2, 3)))
    valid_mask = jnp.arange(SIGNIF, dtype=jnp.int32)[None, :] < counts[:, None]
    kept = jnp.where(valid_mask, weights.astype(jnp.float32), jnp.float32(0.0))
    class_hit = (class_ids[:, :, None] == jnp.arange(CLASSES, dtype=jnp.int32)[None, None, :]).astype(jnp.float32)
    shift_hit = (shift_ids[:, :, None] == jnp.arange(SHIFTS, dtype=jnp.int32)[None, None, :]).astype(jnp.float32)
    mixing = jnp.einsum('ij,ijk,ijs->isk', kept, class_hit, shift_hit).astype(jnp.bfloat16)
    mixing = mixing.reshape(PARTICLES * SHIFTS, CLASSES).astype(jnp.float32)
    flat_images = particles.reshape(ANGLES, PARTICLES * SHIFTS, 2 * CYCLES).astype(jnp.float32)
    class_sums = jnp.einsum('nk,mnc->mkc', mixing, flat_images)
    weight_sums = jnp.einsum('ij,ijk->k', kept, class_hit)
    class_means = class_sums / jnp.maximum(weight_sums, 1.0)[None, :, None]
    return (best_scores, class_means)
```

```python
import functools
import math

import jax
import jax.numpy as jnp
from jax import lax
from jax.experimental import pallas as pl
from jax.experimental.pallas import tpu as pltpu
from jax.sharding import PartitionSpec as P


CHUNK = 16
LANES = 128


def folded_table(angles):
    half = angles // 2
    index = jnp.arange(half, dtype=jnp.int32)
    product = index[:, None] * index[None, :] % angles
    phase = product.astype(jnp.float32) * (2.0 * math.pi / angles)
    edge = (index[:, None] == 0) | (index[None, :] == 0)
    cosine = jnp.cos(phase)
    sine = jnp.where(edge, 0.0, -jnp.sin(phase))
    alternate = jnp.where(index % 2 == 0, 1.0, -1.0)
    nyquist = jnp.where(index[None, :] == 0, alternate[:, None], 0.0)
    last = jnp.concatenate([alternate, jnp.where(index == 0, 1.0, 0.0)])
    rows = [
        jnp.concatenate([cosine, nyquist], axis=1),
        jnp.concatenate([jnp.zeros_like(sine), sine], axis=1),
        jnp.broadcast_to(last[None, :], (8, angles)),
    ]
    return jnp.concatenate(rows, axis=0).astype(jnp.bfloat16)


def score_kernel(scale, rows, shifts, xa, xb, xc, sa, sb, sc, table_ref, out_ref, left_ref, fa, fb, folded):
    step_index = pl.program_id(0)
    lanes = sa.shape[1]
    half = folded.shape[0] // (2 * rows * (lanes // LANES))
    plane = 2 * rows * half
    cycles = LANES // 2
    lane = lax.broadcasted_iota(jnp.int32, (1, LANES), 1)
    sign = jnp.where(lane < cycles, 1.0, -1.0)
    fa[...] = xa[...].astype(jnp.float32)
    fb[pl.ds(0, CHUNK * rows), :] = xb[...].astype(jnp.float32)
    fb[pl.ds(CHUNK * rows, 2 * rows), :] = xc[...].astype(jnp.float32)
    paired = jnp.where(step_index == 0, 0.0, 1.0)
    for t in range(CHUNK):
        a = fa[pl.ds(t * rows, rows), :]
        b = fb[pl.ds((CHUNK - t) * rows, rows), :]
        a_turned = pltpu.roll(a, cycles, 1) * sign
        b_turned = pltpu.roll(b, cycles, 1) * (-sign)
        if t == 0:
            b_turned = b_turned * paired + b * (1.0 - paired)
            a_turned = a_turned * paired
            b = b * paired
        left_ref[pl.ds(0, rows), pl.ds(0, LANES)] = a
        left_ref[pl.ds(0, rows), pl.ds(LANES, LANES)] = b
        left_ref[pl.ds(rows, rows), pl.ds(0, LANES)] = a_turned
        left_ref[pl.ds(rows, rows), pl.ds(LANES, LANES)] = b_turned
        left = left_ref[...].astype(jnp.bfloat16)
        mirrored = sc[0] if t == 0 else sb[CHUNK - t]
        right = jnp.concatenate([sa[t], mirrored], axis=1)
        products = lax.dot_general(
            left, right, (((1,), (1,)), ((), ())), preferred_element_type=jnp.float32
        )
        for v in range(2 * rows // 8):
            for part in range(lanes // LANES):
                folded[pl.ds(part * plane + v * 8 * half + step_index * CHUNK + t, 8, stride=half), :] = products[
                    v * 8 : v * 8 + 8, part * LANES : (part + 1) * LANES
                ]

    @pl.when(step_index == pl.num_programs(0) - 1)
    def _():
        table = table_ref[...]
        each = rows // shifts
        group = 2 * LANES // lanes

        def column(n, part):
            even = folded[pl.ds(pl.multiple_of(part * plane + n * half, half), half), :]
            odd = folded[pl.ds(pl.multiple_of(part * plane + (rows + n) * half, half), half), :]
            return jnp.concatenate([even, odd], axis=0).astype(jnp.bfloat16)

        def one_shift(s, best):
            better = []
            for q in range(each // group):
                columns = [
                    column(s * each + i, part)
                    for i in range(group * q, group * q + group)
                    for part in range(lanes // LANES)
                ]
                turned = jnp.dot(table, jnp.concatenate(columns, axis=1), preferred_element_type=jnp.float32)
                both = turned[:half] + jnp.abs(turned[half : 2 * half])
                top = jnp.max(both.reshape(half // 8, 8, group * lanes), axis=0)
                top = jnp.maximum(top, turned[2 * half :])
                better.append(jnp.maximum(best[q], top))
            return tuple(better)

        start = tuple(jnp.full((8, group * lanes), -jnp.inf, jnp.float32) for _ in range(each // group))
        best = lax.fori_loop(0, shifts, one_shift, start)
        for q in range(each // group):
            top = jnp.max(best[q], axis=0, keepdims=True) * scale
            for i in range(group):
                out_ref[group * q + i : group * q + i + 1, :] = top[:, i * lanes : (i + 1) * lanes]


def best_of_group(lower, upper, upper_offset, stacked, table, shifts, rows, scale):
    angles, lanes, cycle_parts = stacked.shape
    half = angles // 2
    steps = half // CHUNK
    each = rows // shifts
    flops = 2 * half * 2 * rows * 2 * cycle_parts * lanes + 2 * rows * lanes * angles * (angles + 8)
    return pl.pallas_call(
        functools.partial(score_kernel, scale, rows, shifts),
        grid=(steps,),
        in_specs=[
            pl.BlockSpec((CHUNK * rows, cycle_parts), lambda j: (j, 0)),
            pl.BlockSpec((CHUNK * rows, cycle_parts), lambda j: (upper_offset // CHUNK + steps - 1 - j, 0)),
            pl.BlockSpec(
                (2 * rows, cycle_parts),
                lambda j: ((upper_offset + jnp.where(j == 0, 0, half - CHUNK * j)) // 2, 0),
            ),
            pl.BlockSpec((CHUNK, lanes, cycle_parts), lambda j: (j, 0, 0)),
            pl.BlockSpec((CHUNK, lanes, cycle_parts), lambda j: (2 * steps - 1 - j, 0, 0)),
            pl.BlockSpec((1, lanes, cycle_parts), lambda j: (jnp.where(j == 0, half, angles - CHUNK * j), 0, 0)),
            pl.BlockSpec((angles + 8, angles), lambda j: (0, 0)),
        ],
        out_specs=pl.BlockSpec((each, lanes), lambda j: (0, 0)),
        out_shape=jax.ShapeDtypeStruct((each, lanes), jnp.float32),
        scratch_shapes=[
            pltpu.VMEM((2 * rows, 2 * cycle_parts), jnp.float32),
            pltpu.VMEM((CHUNK * rows, cycle_parts), jnp.float32),
            pltpu.VMEM(((CHUNK + 2) * rows, cycle_parts), jnp.float32),
            pltpu.VMEM((2 * rows * half * (lanes // LANES), LANES), jnp.float32),
        ],
        compiler_params=pltpu.CompilerParams(vmem_limit_bytes=48 * 1024 * 1024),
        cost_estimate=pl.CostEstimate(flops=6 * flops, bytes_accessed=30_000_000, transcendentals=0),
        name="score",
    )(lower, upper, upper, stacked, stacked, stacked, table)


def on_device(particles, references, class_ids, counts, shift_ids, weights):
    cls_index = lax.axis_index("cls")
    core = cls_index % 2
    row = cls_index // 2
    angles, own, shifts, cycle_parts = particles.shape
    class_count = references.shape[1]
    list_length = class_ids.shape[1]
    half = angles // 2
    rows = shifts * own
    doms = 32
    chips = 4
    scale = 1.0 / math.sqrt(1.0 * cycle_parts * angles)

    def along(value, step):
        pairs = [(y * 2 + c, (y + step) % chips * 2 + c) for y in range(chips) for c in range(2)]
        return lax.ppermute(value, "cls", pairs)

    def across(value):
        return lax.ppermute(value, "cls", [(i, i ^ 1) for i in range(2 * chips)])

    native = jnp.transpose(particles, (0, 2, 1, 3))
    flat = native.reshape(angles * rows, cycle_parts)
    lower, upper = flat[: half * rows], flat[half * rows :]

    lower_before = along(lower, 1)
    upper_after = along(upper, -1)
    upper_before = along(upper, 1)
    lower_after = along(lower, -1)
    lower_far = along(lower_before, 1)
    upper_far = along(upper_after, -1)

    mate = across(references)
    pad = ((0, 0), (0, LANES // 2 - class_count), (0, 0))
    stacked = jnp.concatenate([jnp.pad(references, pad), jnp.pad(mate, pad)], axis=1)
    table = folded_table(angles)
    score = functools.partial(best_of_group, stacked=stacked, table=table, shifts=shifts, rows=rows, scale=scale)

    listings = own * list_length
    padded = 16
    listed_shift = shift_ids.reshape(listings)
    listed_image = jnp.arange(listings, dtype=jnp.int32) // list_length
    pick = (listed_shift[:, None, None] == jnp.arange(shifts, dtype=jnp.int32)[None, :, None]) & (
        listed_image[:, None, None] == jnp.arange(own, dtype=jnp.int32)[None, None, :]
    )
    pick = jnp.pad(pick.astype(jnp.bfloat16), ((0, padded - listings), (0, 0), (0, 0)))
    listed = jnp.einsum("lsi,msic->mlc", pick, native, preferred_element_type=jnp.float32).astype(jnp.bfloat16)
    valid = jnp.arange(list_length, dtype=jnp.int32)[None, :] < counts[:, None]
    kept = jnp.where(valid, weights, jnp.zeros_like(weights)).reshape(1, listings)
    flat_ids = class_ids.reshape(1, listings)
    notes = jnp.concatenate(
        [(flat_ids // 16).astype(jnp.bfloat16), (flat_ids % 16).astype(jnp.bfloat16), kept], axis=0
    )
    notes = jnp.pad(notes, ((listings, padded - listings - 3), (0, cycle_parts - listings)))
    payload = (listed + notes[None]).reshape(doms, angles // doms, padded, cycle_parts)
    arrived = lax.all_to_all(payload, "dom", 0, 0, tiled=True)
    noted = arrived[:, 0, listings : listings + 3, :listings]
    ids = noted[:, 0].astype(jnp.int32) * 16 + noted[:, 1].astype(jnp.int32)
    classes = 2 * chips * class_count
    hit = ids[None] == jnp.arange(classes, dtype=jnp.int32)[:, None, None]
    mixing = jnp.where(hit, noted[:, 2][None], jnp.zeros((), jnp.bfloat16))
    totals = jnp.sum(mixing.astype(jnp.float32), axis=(1, 2))
    mixing = jnp.pad(mixing, ((0, 0), (0, 0), (0, padded - listings)))
    sums = jnp.einsum("ksl,smlc->kmc", mixing, arrived, preferred_element_type=jnp.float32)
    depth = angles // doms
    sums = sums.reshape(chips, 2, class_count, depth, cycle_parts)
    totals = jnp.pad(totals.reshape(chips, 2, 1, 1, class_count), ((0, 0), (0, 0), (0, 0), (0, depth - 1), (0, cycle_parts - class_count)))
    sums = jnp.concatenate([sums, totals], axis=2)
    mine = lax.dynamic_index_in_dim(sums, core, 1, keepdims=False)
    other = lax.dynamic_index_in_dim(sums, 1 - core, 1, keepdims=False)
    pair_sums = mine + across(other)
    total = lax.dynamic_index_in_dim(pair_sums, row, 0, keepdims=False)
    for step in range(1, chips):
        block = lax.dynamic_index_in_dim(pair_sums, (row + step) % chips, 0, keepdims=False)
        total = total + along(block, step)
    weight_sums = total[class_count, 0, :class_count]
    class_means = total[:class_count] / jnp.maximum(weight_sums, 1.0)[:, None, None]
    class_means = jnp.transpose(class_means, (1, 0, 2))

    own_best = score(flat, flat, half)
    after_best = score(lower_after, upper_after, 0)
    before_best = score(lower_before, upper_before, 0)
    far_best = score(lower_far, upper_far, 0)
    best = jnp.stack([own_best, after_best, far_best, before_best])
    kept_best = best[:, :, :class_count]
    sent_best = across(best[:, :, LANES // 2 : LANES // 2 + class_count])
    first = jnp.where(core == 0, kept_best, sent_best)
    second = jnp.where(core == 0, sent_best, kept_best)
    by_chip = jnp.stack([first, second], axis=1)
    by_chip = jnp.roll(by_chip, row, axis=0)
    best_scores = by_chip.reshape(2 * chips * own, class_count)
    return (best_scores, class_means)


def solution(mesh):
    return jax.shard_map(
        on_device,
        mesh=mesh,
        in_specs=(
            P(None, ("dom", "cls"), None, None),
            P(None, "cls", None),
            P(("dom", "cls"), None),
            P(("dom", "cls")),
            P(("dom", "cls"), None),
            P(("dom", "cls"), None),
        ),
        out_specs=(P("dom", "cls"), P("dom", "cls", None)),
        check_vma=False,
    )
```

```python
import functools
import math

import jax
import jax.numpy as jnp
from jax import lax
from jax.experimental import pallas as pl
from jax.experimental.pallas import tpu as pltpu
from jax.sharding import PartitionSpec as P


CHUNK = 16
LANES = 128
WHOLE = pl.BlockSpec(memory_space=pltpu.VMEM)


def folded_table(angles):
    half = angles // 2
    index = jnp.arange(half, dtype=jnp.int32)
    product = index[:, None] * index[None, :] % angles
    phase = product.astype(jnp.float32) * (2.0 * math.pi / angles)
    edge = (index[:, None] == 0) | (index[None, :] == 0)
    cosine = jnp.cos(phase)
    sine = jnp.where(edge, 0.0, -jnp.sin(phase))
    alternate = jnp.where(index % 2 == 0, 1.0, -1.0)
    nyquist = jnp.where(index[None, :] == 0, alternate[:, None], 0.0)
    last = jnp.concatenate([alternate, jnp.where(index == 0, 1.0, 0.0)])
    rows = [
        jnp.concatenate([cosine, nyquist], axis=1),
        jnp.concatenate([jnp.zeros_like(sine), sine], axis=1),
        jnp.broadcast_to(last[None, :], (8, angles)),
    ]
    return jnp.concatenate(rows, axis=0).astype(jnp.bfloat16)


def gather_kernel(sizes, starts, *refs):
    pieces, out_ref, work = refs[: len(sizes)], refs[len(sizes)], refs[len(sizes) + 1]
    total = out_ref.shape[1]
    work[...] = jnp.zeros(work.shape, jnp.float32)

    def chunk(j, carry):
        base = pl.multiple_of(j * CHUNK, CHUNK)
        for size, start, ref in zip(sizes, starts, pieces):
            block = ref[:, pl.ds(base, CHUNK), :].reshape(size * CHUNK, LANES)
            work[pl.ds(start * CHUNK, size * CHUNK), :] = block.astype(jnp.float32)
        for t in range(CHUNK):
            out_ref[base + t] = work[pl.ds(t, total, stride=CHUNK), :].astype(jnp.bfloat16)
        return carry

    lax.fori_loop(0, out_ref.shape[0] // CHUNK, chunk, 0)


def by_harmonic(pieces, starts):
    angles, cycle_parts = pieces[0].shape[1:]
    sizes = tuple(piece.shape[0] for piece in pieces)
    moved = 2 * angles * cycle_parts * (sum(sizes) + LANES)
    return pl.pallas_call(
        functools.partial(gather_kernel, sizes, tuple(starts)),
        in_specs=[WHOLE] * len(pieces),
        out_specs=WHOLE,
        out_shape=jax.ShapeDtypeStruct((angles, LANES, cycle_parts), jnp.bfloat16),
        scratch_shapes=[pltpu.VMEM((LANES * CHUNK, cycle_parts), jnp.float32)],
        compiler_params=pltpu.CompilerParams(vmem_limit_bytes=30 * 1024 * 1024),
        cost_estimate=pl.CostEstimate(flops=0, bytes_accessed=2 * moved, transcendentals=0),
        name="by_harmonic",
    )(*pieces)


def score_kernel(scale, rows, shifts, half, upper_offset, sets, *refs):
    lower, upper = refs[:2]
    stacked = refs[2 : 2 + sets]
    table_ref, out_ref, left_ref, fa, fb, folded = refs[2 + sets :]
    lanes = sets * LANES
    plane = half * 2 * rows
    cycles = LANES // 2
    lane = lax.broadcasted_iota(jnp.int32, (1, LANES), 1)
    sign = jnp.where(lane < cycles, 1.0, -1.0)
    block = CHUNK * rows

    def chunk(j, carry):
        back = upper_offset + half - CHUNK - j * CHUNK
        edge = jnp.where(j == 0, half, 2 * half - CHUNK * j)
        fa[...] = lower[pl.ds(pl.multiple_of(j * block, block), block), :].astype(jnp.float32)
        fb[pl.ds(0, block), :] = upper[pl.ds(pl.multiple_of(back * rows, block), block), :].astype(jnp.float32)
        edge_rows = pl.multiple_of((edge - half + upper_offset) * rows, block)
        fb[pl.ds(block, 2 * rows), :] = upper[pl.ds(edge_rows, 2 * rows), :].astype(jnp.float32)
        paired = jnp.where(j == 0, 0.0, 1.0)
        for t in range(CHUNK):
            a = fa[pl.ds(t * rows, rows), :]
            b = fb[pl.ds((CHUNK - t) * rows, rows), :]
            a_turned = pltpu.roll(a, cycles, 1) * sign
            b_turned = pltpu.roll(b, cycles, 1) * (-sign)
            if t == 0:
                b_turned = b_turned * paired + b * (1.0 - paired)
                a_turned = a_turned * paired
                b = b * paired
            slot = t % left_ref.shape[0]
            left_ref[slot, pl.ds(0, rows), pl.ds(0, LANES)] = a
            left_ref[slot, pl.ds(0, rows), pl.ds(LANES, LANES)] = b
            left_ref[slot, pl.ds(rows, rows), pl.ds(0, LANES)] = a_turned
            left_ref[slot, pl.ds(rows, rows), pl.ds(LANES, LANES)] = b_turned
            m = j * CHUNK + t
            mirror = edge if t == 0 else 2 * half - m
            right = jnp.concatenate(
                [
                    jnp.concatenate([ref[m] for ref in stacked], axis=0),
                    jnp.concatenate([ref[mirror] for ref in stacked], axis=0),
                ],
                axis=1,
            )
            products = lax.dot_general(
                left_ref[slot].astype(jnp.bfloat16),
                right,
                (((1,), (1,)), ((), ())),
                preferred_element_type=jnp.float32,
            )
            for part in range(sets):
                first = pl.multiple_of(part * plane + m * 2 * rows, 8)
                folded[pl.ds(first, 2 * rows), :] = products[:, part * LANES : (part + 1) * LANES]
        return carry

    lax.fori_loop(0, half // CHUNK, chunk, 0)
    table = table_ref[...]
    each = rows // shifts
    group = 2 // sets
    width = 2 * LANES

    def column(n, part):
        even = folded[pl.ds(part * plane + n, half, stride=2 * rows), :]
        odd = folded[pl.ds(part * plane + rows + n, half, stride=2 * rows), :]
        return jnp.concatenate([even, odd], axis=0).astype(jnp.bfloat16)

    def one_shift(s, best):
        better = []
        for q in range(each // group):
            columns = [
                column(s * each + i, part) for i in range(group * q, group * q + group) for part in range(sets)
            ]
            turned = jnp.dot(table, jnp.concatenate(columns, axis=1), preferred_element_type=jnp.float32)
            both = turned[:half] + jnp.abs(turned[half : 2 * half])
            top = jnp.max(both.reshape(half // 8, 8, width), axis=0)
            top = jnp.maximum(top, turned[2 * half :])
            better.append(jnp.maximum(best[q], top))
        return tuple(better)

    start = tuple(jnp.full((8, width), -jnp.inf, jnp.float32) for _ in range(each // group))
    best = lax.fori_loop(0, shifts, one_shift, start)
    for q in range(each // group):
        top = jnp.max(best[q], axis=0, keepdims=True) * scale
        for i in range(group):
            out_ref[group * q + i : group * q + i + 1, :] = top[:, i * lanes : (i + 1) * lanes]


def best_of_group(lower, upper, upper_offset, stacked, table, shifts, rows, scale):
    angles, _, cycle_parts = stacked[0].shape
    half = angles // 2
    each = rows // shifts
    sets = len(stacked)
    lanes = sets * LANES
    flops = 2 * half * 2 * rows * 2 * cycle_parts * lanes + 2 * rows * lanes * angles * (angles + 8)
    return pl.pallas_call(
        functools.partial(score_kernel, scale, rows, shifts, half, upper_offset, sets),
        in_specs=[WHOLE] * (3 + sets),
        out_specs=WHOLE,
        out_shape=jax.ShapeDtypeStruct((each, lanes), jnp.float32),
        scratch_shapes=[
            pltpu.VMEM((4, 2 * rows, 2 * cycle_parts), jnp.float32),
            pltpu.VMEM((CHUNK * rows, cycle_parts), jnp.float32),
            pltpu.VMEM(((CHUNK + 2) * rows, cycle_parts), jnp.float32),
            pltpu.VMEM((sets * 2 * rows * half, LANES), jnp.float32),
        ],
        compiler_params=pltpu.CompilerParams(vmem_limit_bytes=32 * 1024 * 1024),
        cost_estimate=pl.CostEstimate(flops=6 * flops, bytes_accessed=20_000_000, transcendentals=0),
        name="score",
    )(lower, upper, *stacked, table)


def on_device(particles, references, class_ids, counts, shift_ids, weights):
    cls_index = lax.axis_index("cls")
    core = cls_index % 2
    row = cls_index // 2
    angles, own, shifts, cycle_parts = particles.shape
    class_count = references.shape[1]
    list_length = class_ids.shape[1]
    half = angles // 2
    rows = shifts * own
    doms = 32
    chips = 4
    scale = 1.0 / math.sqrt(1.0 * cycle_parts * angles)

    def along(value, step):
        pairs = [(y * 2 + c, (y + step) % chips * 2 + c) for y in range(chips) for c in range(2)]
        return lax.ppermute(value, "cls", pairs)

    def across(value):
        return lax.ppermute(value, "cls", [(i, i ^ 1) for i in range(2 * chips)])

    native = jnp.transpose(particles, (0, 2, 1, 3))
    flat = native.reshape(angles * rows, cycle_parts)

    before = along(flat, 1)
    after = along(flat, -1)
    lower_far = along(before[: half * rows], 1)
    upper_far = along(after[half * rows :], -1)

    class_major = jnp.transpose(references, (1, 0, 2))
    mate = across(class_major)
    stacked = (by_harmonic([class_major, mate], [0, LANES // 2]),)
    table = folded_table(angles)
    score = functools.partial(best_of_group, stacked=stacked, table=table, shifts=shifts, rows=rows, scale=scale)

    listings = own * list_length
    padded = 16
    listed_shift = shift_ids.reshape(listings)
    listed_image = jnp.arange(listings, dtype=jnp.int32) // list_length
    pick = (listed_shift[:, None, None] == jnp.arange(shifts, dtype=jnp.int32)[None, :, None]) & (
        listed_image[:, None, None] == jnp.arange(own, dtype=jnp.int32)[None, None, :]
    )
    pick = jnp.pad(pick.astype(jnp.bfloat16), ((0, padded - listings), (0, 0), (0, 0)))
    listed = jnp.einsum("lsi,msic->mlc", pick, native, preferred_element_type=jnp.float32).astype(jnp.bfloat16)
    valid = jnp.arange(list_length, dtype=jnp.int32)[None, :] < counts[:, None]
    kept = jnp.where(valid, weights, jnp.zeros_like(weights)).reshape(1, listings)
    flat_ids = class_ids.reshape(1, listings)
    notes = jnp.concatenate(
        [(flat_ids // 16).astype(jnp.bfloat16), (flat_ids % 16).astype(jnp.bfloat16), kept], axis=0
    )
    notes = jnp.pad(notes, ((listings, padded - listings - 3), (0, cycle_parts - listings)))
    payload = (listed + notes[None]).reshape(doms, angles // doms, padded, cycle_parts)
    arrived = lax.all_to_all(payload, "dom", 0, 0, tiled=True)
    noted = arrived[:, 0, listings : listings + 3, :listings]
    ids = noted[:, 0].astype(jnp.int32) * 16 + noted[:, 1].astype(jnp.int32)
    classes = 2 * chips * class_count
    hit = ids[None] == jnp.arange(classes, dtype=jnp.int32)[:, None, None]
    mixing = jnp.where(hit, noted[:, 2][None], jnp.zeros((), jnp.bfloat16))
    totals = jnp.sum(mixing.astype(jnp.float32), axis=(1, 2))
    mixing = jnp.pad(mixing, ((0, 0), (0, 0), (0, padded - listings)))
    sums = jnp.einsum("ksl,smlc->kmc", mixing, arrived, preferred_element_type=jnp.float32)
    depth = angles // doms
    sums = sums.reshape(chips, 2, class_count, depth, cycle_parts)
    totals = jnp.pad(totals.reshape(chips, 2, 1, 1, class_count), ((0, 0), (0, 0), (0, 0), (0, depth - 1), (0, cycle_parts - class_count)))
    sums = jnp.concatenate([sums, totals], axis=2)
    mine = lax.dynamic_index_in_dim(sums, core, 1, keepdims=False)
    other = lax.dynamic_index_in_dim(sums, 1 - core, 1, keepdims=False)
    pair_sums = mine + across(other)
    total = lax.dynamic_index_in_dim(pair_sums, row, 0, keepdims=False)
    for step in range(1, chips):
        block = lax.dynamic_index_in_dim(pair_sums, (row + step) % chips, 0, keepdims=False)
        total = total + along(block, step)
    weight_sums = total[class_count, 0, :class_count]
    class_means = total[:class_count] / jnp.maximum(weight_sums, 1.0)[:, None, None]
    class_means = jnp.transpose(class_means, (1, 0, 2))

    own_best = score(flat, flat, half)
    after_best = score(after, after, half)
    before_best = score(before, before, half)
    far_best = score(lower_far, upper_far, 0)
    best = jnp.stack([own_best, after_best, far_best, before_best])
    kept_best = best[:, :, :class_count]
    sent_best = across(best[:, :, LANES // 2 : LANES // 2 + class_count])
    first = jnp.where(core == 0, kept_best, sent_best)
    second = jnp.where(core == 0, sent_best, kept_best)
    by_chip = jnp.stack([first, second], axis=1)
    by_chip = jnp.roll(by_chip, row, axis=0)
    best_scores = by_chip.reshape(2 * chips * own, class_count)
    return (best_scores, class_means)


def solution(mesh):
    return jax.shard_map(
        on_device,
        mesh=mesh,
        in_specs=(
            P(None, ("dom", "cls"), None, None),
            P(None, "cls", None),
            P(("dom", "cls"), None),
            P(("dom", "cls")),
            P(("dom", "cls"), None),
            P(("dom", "cls"), None),
        ),
        out_specs=(P("dom", "cls"), P("dom", "cls", None)),
        check_vma=False,
    )
```

```python
import functools
import math

import jax
import jax.numpy as jnp
from jax import lax
from jax.experimental import pallas as pl
from jax.experimental.pallas import tpu as pltpu
from jax.sharding import PartitionSpec as P


CHUNK = 16
LANES = 128
WHOLE = pl.BlockSpec(memory_space=pltpu.VMEM)


def folded_table(angles):
    half = angles // 2
    index = jnp.arange(half, dtype=jnp.int32)
    product = index[:, None] * index[None, :] % angles
    phase = product.astype(jnp.float32) * (2.0 * math.pi / angles)
    edge = (index[:, None] == 0) | (index[None, :] == 0)
    cosine = jnp.cos(phase)
    sine = jnp.where(edge, 0.0, -jnp.sin(phase))
    alternate = jnp.where(index % 2 == 0, 1.0, -1.0)
    nyquist = jnp.where(index[None, :] == 0, alternate[:, None], 0.0)
    last = jnp.concatenate([alternate, jnp.where(index == 0, 1.0, 0.0)])
    rows = [
        jnp.concatenate([cosine, nyquist], axis=1),
        jnp.concatenate([jnp.zeros_like(sine), sine], axis=1),
        jnp.broadcast_to(last[None, :], (8, angles)),
    ]
    return jnp.concatenate(rows, axis=0).astype(jnp.bfloat16)


def gather_kernel(sizes, starts, *refs):
    pieces, out_ref, work = refs[: len(sizes)], refs[len(sizes)], refs[len(sizes) + 1]
    total = out_ref.shape[1]
    work[...] = jnp.zeros(work.shape, jnp.float32)

    def chunk(j, carry):
        base = pl.multiple_of(j * CHUNK, CHUNK)
        for size, start, ref in zip(sizes, starts, pieces):
            block = ref[:, pl.ds(base, CHUNK), :].reshape(size * CHUNK, LANES)
            work[pl.ds(start * CHUNK, size * CHUNK), :] = block.astype(jnp.float32)
        for t in range(CHUNK):
            out_ref[base + t] = work[pl.ds(t, total, stride=CHUNK), :].astype(jnp.bfloat16)
        return carry

    lax.fori_loop(0, out_ref.shape[0] // CHUNK, chunk, 0)


def by_harmonic(pieces, starts, total):
    angles, cycle_parts = pieces[0].shape[1:]
    sizes = tuple(piece.shape[0] for piece in pieces)
    moved = 2 * angles * cycle_parts * (sum(sizes) + total)
    return pl.pallas_call(
        functools.partial(gather_kernel, sizes, tuple(starts)),
        in_specs=[WHOLE] * len(pieces),
        out_specs=WHOLE,
        out_shape=jax.ShapeDtypeStruct((angles, total, cycle_parts), jnp.bfloat16),
        scratch_shapes=[pltpu.VMEM((total * CHUNK, cycle_parts), jnp.float32)],
        compiler_params=pltpu.CompilerParams(vmem_limit_bytes=30 * 1024 * 1024),
        cost_estimate=pl.CostEstimate(flops=0, bytes_accessed=2 * moved, transcendentals=0),
        name="by_harmonic",
    )(*pieces)


def score_kernel(scale, rows, shifts, groups, *refs):
    images, stacked = refs[:groups], refs[groups : groups + 2]
    table_ref, out_ref, left_ref, fa, fb, folded = refs[groups + 2 :]
    half = table_ref.shape[1] // 2
    all_rows = 2 * rows * groups
    cycles = LANES // 2
    lane = lax.broadcasted_iota(jnp.int32, (1, LANES), 1)
    sign = jnp.where(lane < cycles, 1.0, -1.0)
    block = CHUNK * rows

    def chunk(j, carry):
        back = 2 * half - CHUNK - j * CHUNK
        edge = jnp.where(j == 0, half, 2 * half - CHUNK * j)
        for g, image in enumerate(images):
            fa[g] = image[pl.ds(pl.multiple_of(j * block, block), block), :].astype(jnp.float32)
            fb[g, pl.ds(0, block), :] = image[pl.ds(pl.multiple_of(back * rows, block), block), :].astype(jnp.float32)
            edge_rows = pl.multiple_of(edge * rows, block)
            fb[g, pl.ds(block, 2 * rows), :] = image[pl.ds(edge_rows, 2 * rows), :].astype(jnp.float32)
        paired = jnp.where(j == 0, 0.0, 1.0)
        for t in range(CHUNK):
            slot = t % left_ref.shape[0]
            for g in range(groups):
                a = fa[g, pl.ds(t * rows, rows), :]
                b = fb[g, pl.ds((CHUNK - t) * rows, rows), :]
                a_turned = pltpu.roll(a, cycles, 1) * sign
                b_turned = pltpu.roll(b, cycles, 1) * (-sign)
                if t == 0:
                    b_turned = b_turned * paired + b * (1.0 - paired)
                    a_turned = a_turned * paired
                    b = b * paired
                top = 2 * rows * g
                left_ref[slot, pl.ds(top, rows), pl.ds(0, LANES)] = a
                left_ref[slot, pl.ds(top, rows), pl.ds(LANES, LANES)] = b
                left_ref[slot, pl.ds(top + rows, rows), pl.ds(0, LANES)] = a_turned
                left_ref[slot, pl.ds(top + rows, rows), pl.ds(LANES, LANES)] = b_turned
            m = j * CHUNK + t
            mirror = edge if t == 0 else 2 * half - m
            right = jnp.concatenate(
                [
                    jnp.concatenate([ref[m] for ref in stacked], axis=0),
                    jnp.concatenate([ref[mirror] for ref in stacked], axis=0),
                ],
                axis=1,
            )
            folded[pl.ds(pl.multiple_of(m * all_rows, 8), all_rows), :] = lax.dot_general(
                left_ref[slot].astype(jnp.bfloat16),
                right,
                (((1,), (1,)), ((), ())),
                preferred_element_type=jnp.float32,
            )
        return carry

    lax.fori_loop(0, half // CHUNK, chunk, 0)
    table = table_ref[...]
    each = rows // shifts
    width = 2 * LANES

    def column(g, n):
        even = folded[pl.ds(2 * rows * g + n, half, stride=all_rows), :]
        odd = folded[pl.ds(2 * rows * g + rows + n, half, stride=all_rows), :]
        return jnp.concatenate([even, odd], axis=0).astype(jnp.bfloat16)

    def one_shift(s, best):
        better = []
        for q in range(groups * each // 2):
            columns = [column(i // each, s * each + i % each) for i in (2 * q, 2 * q + 1)]
            turned = jnp.dot(table, jnp.concatenate(columns, axis=1), preferred_element_type=jnp.float32)
            both = turned[:half] + jnp.abs(turned[half : 2 * half])
            top = jnp.max(both.reshape(half // 8, 8, width), axis=0)
            top = jnp.maximum(top, turned[2 * half :])
            better.append(jnp.maximum(best[q], top))
        return tuple(better)

    start = tuple(jnp.full((8, width), -jnp.inf, jnp.float32) for _ in range(groups * each // 2))
    best = lax.fori_loop(0, shifts, one_shift, start)
    for q in range(groups * each // 2):
        top = jnp.max(best[q], axis=0, keepdims=True) * scale
        out_ref[2 * q : 2 * q + 1, :] = top[:, :LANES]
        out_ref[2 * q + 1 : 2 * q + 2, :] = top[:, LANES:]


def best_of_groups(images, stacked, table, shifts, rows, scale):
    angles, _, cycle_parts = stacked[0].shape
    half = angles // 2
    each = rows // shifts
    groups = len(images)
    flops = groups * (2 * half * 2 * rows * 2 * cycle_parts * LANES + 2 * rows * LANES * angles * (angles + 8))
    return pl.pallas_call(
        functools.partial(score_kernel, scale, rows, shifts, groups),
        in_specs=[WHOLE] * (groups + 3),
        out_specs=WHOLE,
        out_shape=jax.ShapeDtypeStruct((groups * each, LANES), jnp.float32),
        scratch_shapes=[
            pltpu.VMEM((4, 2 * rows * groups, 2 * cycle_parts), jnp.float32),
            pltpu.VMEM((groups, CHUNK * rows, cycle_parts), jnp.float32),
            pltpu.VMEM((groups, (CHUNK + 2) * rows, cycle_parts), jnp.float32),
            pltpu.VMEM((2 * rows * groups * half, LANES), jnp.float32),
        ],
        compiler_params=pltpu.CompilerParams(vmem_limit_bytes=34 * 1024 * 1024),
        cost_estimate=pl.CostEstimate(flops=6 * flops, bytes_accessed=20_000_000, transcendentals=0),
        name="score",
    )(*images, *stacked, table)


def on_device(particles, references, class_ids, counts, shift_ids, weights):
    cls_index = lax.axis_index("cls")
    core = cls_index % 2
    row = cls_index // 2
    angles, own, shifts, cycle_parts = particles.shape
    class_count = references.shape[1]
    list_length = class_ids.shape[1]
    rows = shifts * own
    doms = 32
    chips = 4
    ring = 4
    scale = 1.0 / math.sqrt(1.0 * cycle_parts * angles)

    def move(value, target):
        pairs = [(2 * y + c, 2 * t + e) for y in range(chips) for c in range(2) for t, e in [target(y, c)]]
        return lax.ppermute(value, "cls", pairs)

    def along(value, step):
        return move(value, lambda y, c: ((y + step) % chips, c))

    def across(value):
        return move(value, lambda y, c: (y, 1 - c))

    def facing(value):
        return move(value, lambda y, c: (chips - 1 - y, c))

    def around(value, step):
        length = doms // ring
        pairs = [(x * length + z, (x + step) % ring * length + z) for x in range(ring) for z in range(length)]
        return lax.ppermute(value, "dom", pairs)

    native = jnp.transpose(particles, (0, 2, 1, 3))
    flat = native.reshape(angles * rows, cycle_parts)
    class_major = jnp.transpose(references, (1, 0, 2))

    place = lax.axis_index("dom") // (doms // ring)
    straight = 20
    window = -(-(class_count - straight) // ring)
    first = jnp.minimum(straight + window * place, class_count - window)
    piece = facing(lax.dynamic_slice_in_dim(class_major, first, window, 0))
    direct = facing(class_major[:straight])
    from_left = around(piece, 1)
    from_right = around(piece, -1)
    far_upper = around(from_left[: window // 2], 1)
    far_lower = around(from_right[window // 2 :], -1)

    partner = move(flat, lambda y, c: (y ^ 1, c))
    mate = across(flat)
    partner_mate = across(partner)

    own_set = by_harmonic([class_major], [0], LANES // 2)
    starts = [0, straight, straight + window, straight + 2 * window, straight + 3 * window, straight + 3 * window + window // 2]
    facing_set = by_harmonic([direct, piece, from_left, from_right, far_upper, far_lower], starts, LANES // 2)
    stacked = [own_set, facing_set]
    table = folded_table(angles)
    score = functools.partial(best_of_groups, stacked=stacked, table=table, shifts=shifts, rows=rows, scale=scale)

    listings = own * list_length
    padded = 16
    listed_shift = shift_ids.reshape(listings)
    listed_image = jnp.arange(listings, dtype=jnp.int32) // list_length
    pick = (listed_shift[:, None, None] == jnp.arange(shifts, dtype=jnp.int32)[None, :, None]) & (
        listed_image[:, None, None] == jnp.arange(own, dtype=jnp.int32)[None, None, :]
    )
    pick = jnp.pad(pick.astype(jnp.bfloat16), ((0, padded - listings), (0, 0), (0, 0)))
    listed = jnp.einsum("lsi,msic->mlc", pick, native, preferred_element_type=jnp.float32).astype(jnp.bfloat16)
    valid = jnp.arange(list_length, dtype=jnp.int32)[None, :] < counts[:, None]
    kept = jnp.where(valid, weights, jnp.zeros_like(weights)).reshape(1, listings)
    flat_ids = class_ids.reshape(1, listings)
    notes = jnp.concatenate(
        [(flat_ids // 16).astype(jnp.bfloat16), (flat_ids % 16).astype(jnp.bfloat16), kept], axis=0
    )
    notes = jnp.pad(notes, ((listings, padded - listings - 3), (0, cycle_parts - listings)))
    payload = (listed + notes[None]).reshape(doms, angles // doms, padded, cycle_parts)
    arrived = lax.all_to_all(payload, "dom", 0, 0, tiled=True)
    noted = arrived[:, 0, listings : listings + 3, :listings]
    ids = noted[:, 0].astype(jnp.int32) * 16 + noted[:, 1].astype(jnp.int32)
    classes = 2 * chips * class_count
    hit = ids[None] == jnp.arange(classes, dtype=jnp.int32)[:, None, None]
    mixing = jnp.where(hit, noted[:, 2][None], jnp.zeros((), jnp.bfloat16))
    totals = jnp.sum(mixing.astype(jnp.float32), axis=(1, 2))
    mixing = jnp.pad(mixing, ((0, 0), (0, 0), (0, padded - listings)))
    sums = jnp.einsum("ksl,smlc->kmc", mixing, arrived, preferred_element_type=jnp.float32)
    depth = angles // doms
    sums = sums.reshape(chips, 2, class_count, depth, cycle_parts)
    totals = jnp.pad(totals.reshape(chips, 2, 1, 1, class_count), ((0, 0), (0, 0), (0, 0), (0, depth - 1), (0, cycle_parts - class_count)))
    sums = jnp.concatenate([sums, totals], axis=2)
    mine = lax.dynamic_index_in_dim(sums, core, 1, keepdims=False)
    other = lax.dynamic_index_in_dim(sums, 1 - core, 1, keepdims=False)
    pair_sums = mine + across(other)
    total = lax.dynamic_index_in_dim(pair_sums, row, 0, keepdims=False)
    for step in range(1, chips):
        block = lax.dynamic_index_in_dim(pair_sums, (row + step) % chips, 0, keepdims=False)
        total = total + along(block, step)
    weight_sums = total[class_count, 0, :class_count]
    class_means = total[:class_count] / jnp.maximum(weight_sums, 1.0)[:, None, None]
    class_means = jnp.transpose(class_means, (1, 0, 2))

    home = score([flat, mate])
    away = score([partner, partner_mate])
    best = jnp.concatenate([home, away], axis=0)
    lanes_of = LANES // 2
    sent = facing(best[:, lanes_of : lanes_of + straight + ring * window])
    by_step = [sent[:, straight + window * k : straight + window * (k + 1)] for k in (0, 2, 3, 1)]
    overlap = straight + ring * window - class_count
    ordered = []
    for x in range(ring):
        columns = [by_step[(k - x) % ring] for k in range(ring)]
        columns[-1] = columns[-1][:, overlap:]
        ordered.append(jnp.concatenate([sent[:, :straight]] + columns, axis=1))
    others = lax.select_n(place, *ordered)
    own_best = best[:, :class_count].reshape(2, 2, own, class_count)
    facing_best = others.reshape(2, 2, own, class_count)
    grid = jnp.stack([own_best, facing_best[::-1]])
    for axis, bit in ((0, row // 2), (1, row % 2), (2, core)):
        grid = jnp.where(bit == 1, jnp.flip(grid, axis), grid)
    best_scores = grid.reshape(2 * chips * own, class_count)
    return (best_scores, class_means)


def solution(mesh):
    return jax.shard_map(
        on_device,
        mesh=mesh,
        in_specs=(
            P(None, ("dom", "cls"), None, None),
            P(None, "cls", None),
            P(("dom", "cls"), None),
            P(("dom", "cls")),
            P(("dom", "cls"), None),
            P(("dom", "cls"), None),
        ),
        out_specs=(P("dom", "cls"), P("dom", "cls", None)),
        check_vma=False,
    )
```

```python
import functools
import math

import jax
import jax.numpy as jnp
from jax import lax
from jax.experimental import pallas as pl
from jax.experimental.pallas import tpu as pltpu
from jax.sharding import PartitionSpec as P


CHUNK = 16
LANES = 128
WHOLE = pl.BlockSpec(memory_space=pltpu.VMEM)
SCALARS = pl.BlockSpec(memory_space=pltpu.SMEM)


def folded_table(angles):
    half = angles // 2
    index = jnp.arange(half, dtype=jnp.int32)
    product = index[:, None] * index[None, :] % angles
    phase = product.astype(jnp.float32) * (2.0 * math.pi / angles)
    edge = (index[:, None] == 0) | (index[None, :] == 0)
    cosine = jnp.cos(phase)
    sine = jnp.where(edge, 0.0, -jnp.sin(phase))
    alternate = jnp.where(index % 2 == 0, 1.0, -1.0)
    nyquist = jnp.where(index[None, :] == 0, alternate[:, None], 0.0)
    last = jnp.concatenate([alternate, jnp.where(index == 0, 1.0, 0.0)])
    rows = [
        jnp.concatenate([cosine, nyquist], axis=1),
        jnp.concatenate([jnp.zeros_like(sine), sine], axis=1),
        jnp.broadcast_to(last[None, :], (8, angles)),
    ]
    return jnp.concatenate(rows, axis=0).astype(jnp.bfloat16)


def gather_kernel(sizes, starts_ref, *refs):
    pieces, out_ref, work = refs[: len(sizes)], refs[len(sizes)], refs[len(sizes) + 1]
    total = out_ref.shape[1]
    used = sum(sizes)
    work[pl.ds(used * CHUNK, (total - used) * CHUNK), :] = jnp.zeros(((total - used) * CHUNK, LANES), jnp.float32)

    def chunk(j, carry):
        base = pl.multiple_of(j * CHUNK, CHUNK)
        for k, (size, ref) in enumerate(zip(sizes, pieces)):
            block = ref[:, pl.ds(base, CHUNK), :].reshape(size * CHUNK, LANES)
            first = pl.multiple_of(starts_ref[k] * CHUNK, CHUNK)
            work[pl.ds(first, size * CHUNK), :] = block.astype(jnp.float32)
        for t in range(CHUNK):
            out_ref[base + t] = work[pl.ds(t, total, stride=CHUNK), :].astype(jnp.bfloat16)
        return carry

    lax.fori_loop(0, out_ref.shape[0] // CHUNK, chunk, 0)


def by_harmonic(pieces, starts, total):
    angles, cycle_parts = pieces[0].shape[1:]
    sizes = tuple(piece.shape[0] for piece in pieces)
    moved = 2 * angles * cycle_parts * (sum(sizes) + total)
    return pl.pallas_call(
        functools.partial(gather_kernel, sizes),
        in_specs=[SCALARS] + [WHOLE] * len(pieces),
        out_specs=WHOLE,
        out_shape=jax.ShapeDtypeStruct((angles, total, cycle_parts), jnp.bfloat16),
        scratch_shapes=[pltpu.VMEM((total * CHUNK, cycle_parts), jnp.float32)],
        compiler_params=pltpu.CompilerParams(vmem_limit_bytes=14 * 1024 * 1024),
        cost_estimate=pl.CostEstimate(flops=0, bytes_accessed=2 * moved, transcendentals=0),
        name="by_harmonic",
    )(jnp.asarray(starts, jnp.int32), *pieces)


def score_kernel(scale, rows, shifts, counts, places_ref, *refs):
    groups, pieces = len(counts), sum(counts)
    firsts = [sum(counts[:g]) for g in range(groups)]
    lowers = [refs[first] for first in firsts]
    uppers = [refs[first + count - 1] for first, count in zip(firsts, counts)]
    stacked = refs[pieces : pieces + 2]
    table_ref, out_ref, left_ref, fa, fb, folded = refs[pieces + 2 :]
    half = table_ref.shape[1] // 2
    all_rows = 2 * rows * groups
    pitch = all_rows + 1
    cycles = LANES // 2
    lane = lax.broadcasted_iota(jnp.int32, (1, LANES), 1)
    sign = jnp.where(lane < cycles, 1.0, -1.0)
    block = CHUNK * rows

    def chunk(j, carry):
        back = 2 * half - CHUNK - j * CHUNK
        edge = jnp.where(j == 0, half, 2 * half - CHUNK * j)
        for g, (lower, upper) in enumerate(zip(lowers, uppers)):
            skip = upper.shape[0] // rows - 2 * half
            fa[g] = lower[pl.ds(pl.multiple_of(j * block, block), block), :].astype(jnp.float32)
            back_rows = pl.multiple_of((back + skip) * rows, block)
            fb[g, pl.ds(0, block), :] = upper[pl.ds(back_rows, block), :].astype(jnp.float32)
            edge_rows = pl.multiple_of((edge + skip) * rows, block)
            fb[g, pl.ds(block, 2 * rows), :] = upper[pl.ds(edge_rows, 2 * rows), :].astype(jnp.float32)
        paired = jnp.where(j == 0, 0.0, 1.0)
        for t in range(CHUNK):
            slot = t % left_ref.shape[0]
            for g in range(groups):
                a = fa[g, pl.ds(t * rows, rows), :]
                b = fb[g, pl.ds((CHUNK - t) * rows, rows), :]
                a_turned = pltpu.roll(a, cycles, 1) * sign
                b_turned = pltpu.roll(b, cycles, 1) * (-sign)
                if t == 0:
                    b_turned = b_turned * paired + b * (1.0 - paired)
                    a_turned = a_turned * paired
                    b = b * paired
                top = 2 * rows * g
                left_ref[slot, pl.ds(top, rows), pl.ds(0, LANES)] = a
                left_ref[slot, pl.ds(top, rows), pl.ds(LANES, LANES)] = b
                left_ref[slot, pl.ds(top + rows, rows), pl.ds(0, LANES)] = a_turned
                left_ref[slot, pl.ds(top + rows, rows), pl.ds(LANES, LANES)] = b_turned
            m = j * CHUNK + t
            mirror = edge if t == 0 else 2 * half - m
            right = jnp.concatenate(
                [
                    jnp.concatenate([ref[m] for ref in stacked], axis=0),
                    jnp.concatenate([ref[mirror] for ref in stacked], axis=0),
                ],
                axis=1,
            )
            folded[pl.ds(m * pitch, all_rows), :] = lax.dot_general(
                left_ref[slot].astype(jnp.bfloat16),
                right,
                (((1,), (1,)), ((), ())),
                preferred_element_type=jnp.float32,
            )
        return carry

    lax.fori_loop(0, half // CHUNK, chunk, 0)
    table = table_ref[...]
    each = rows // shifts
    width = 2 * LANES

    def column(g, n):
        even = folded[pl.ds(2 * rows * g + n, half, stride=pitch), :]
        odd = folded[pl.ds(2 * rows * g + rows + n, half, stride=pitch), :]
        return jnp.concatenate([even, odd], axis=0).astype(jnp.bfloat16)

    def one_shift(s, best):
        better = []
        for q in range(groups * each // 2):
            columns = [column(i // each, s * each + i % each) for i in (2 * q, 2 * q + 1)]
            turned = jnp.dot(table, jnp.concatenate(columns, axis=1), preferred_element_type=jnp.float32)
            both = turned[:half] + jnp.abs(turned[half : 2 * half])
            top = jnp.max(both.reshape(half // 8, 8, width), axis=0)
            top = jnp.maximum(top, turned[2 * half :])
            better.append(jnp.maximum(best[q], top))
        return tuple(better)

    start = tuple(jnp.full((8, width), -jnp.inf, jnp.float32) for _ in range(groups * each // 2))
    best = lax.fori_loop(0, shifts, one_shift, start)
    for q in range(groups * each // 2):
        top = jnp.max(best[q], axis=0, keepdims=True) * scale
        first = places_ref[2 * q // each] * each + 2 * q % each
        out_ref[pl.ds(first, 1), :] = top[:, :LANES]
        out_ref[pl.ds(first + 1, 1), :] = top[:, LANES:]


def best_of_groups(places, images, stacked, table, shifts, rows, scale):
    angles, _, cycle_parts = stacked[0].shape
    half = angles // 2
    each = rows // shifts
    groups = len(images)
    counts = tuple(len(image) for image in images)
    flops = groups * (2 * half * 2 * rows * 2 * cycle_parts * LANES + 2 * rows * LANES * angles * (angles + 8))
    return pl.pallas_call(
        functools.partial(score_kernel, scale, rows, shifts, counts),
        in_specs=[SCALARS] + [WHOLE] * (sum(counts) + 3),
        out_specs=WHOLE,
        out_shape=jax.ShapeDtypeStruct((groups * each, LANES), jnp.float32),
        scratch_shapes=[
            pltpu.VMEM((4, 2 * rows * groups, 2 * cycle_parts), jnp.float32),
            pltpu.VMEM((groups, CHUNK * rows, cycle_parts), jnp.float32),
            pltpu.VMEM((groups, (CHUNK + 2) * rows, cycle_parts), jnp.float32),
            pltpu.VMEM(((2 * rows * groups + 1) * half, LANES), jnp.float32),
        ],
        compiler_params=pltpu.CompilerParams(vmem_limit_bytes=36 * 1024 * 1024),
        cost_estimate=pl.CostEstimate(flops=6 * flops, bytes_accessed=20_000_000, transcendentals=0),
        name="score",
    )(places, *[piece for image in images for piece in image], *stacked, table)


def on_device(particles, references, class_ids, counts, shift_ids, weights):
    cls_index = lax.axis_index("cls")
    core = cls_index % 2
    row = cls_index // 2
    angles, own, shifts, cycle_parts = particles.shape
    class_count = references.shape[1]
    list_length = class_ids.shape[1]
    half = angles // 2
    rows = shifts * own
    doms = 32
    chips = 4
    ring = 4
    scale = 1.0 / math.sqrt(1.0 * cycle_parts * angles)

    def move(value, target):
        pairs = [(2 * y + c, 2 * t + e) for y in range(chips) for c in range(2) for t, e in [target(y, c)]]
        return lax.ppermute(value, "cls", pairs)

    def along(value, step):
        return move(value, lambda y, c: ((y + step) % chips, c))

    def across(value):
        return move(value, lambda y, c: (y, 1 - c))

    def facing(value):
        return move(value, lambda y, c: (chips - 1 - y, c))

    def around(value, step):
        length = doms // ring
        pairs = [(x * length + z, (x + step) % ring * length + z) for x in range(ring) for z in range(length)]
        return lax.ppermute(value, "dom", pairs)

    native = jnp.transpose(particles, (0, 2, 1, 3))
    flat = native.reshape(angles * rows, cycle_parts)
    class_major = jnp.transpose(references, (1, 0, 2))

    lower, again = lax.optimization_barrier((flat[: half * rows], flat))
    upper = again[half * rows :]
    lower_partner = move(lower, lambda y, c: (y ^ 1, c))
    upper_partner = move(upper, lambda y, c: (y ^ 1, c))
    mate = across(flat)
    lower_both = across(lower_partner)
    upper_both = across(upper_partner)

    place = lax.axis_index("dom") // (doms // ring)
    window = class_count // (ring + 1)
    straight = class_count - ring * window

    def window_of(x):
        return lax.dynamic_slice_in_dim(class_major, straight + window * x, window, 0)

    piece = facing(window_of(place))
    far = facing(jnp.concatenate([class_major[:straight], window_of((place + 2) % ring)]))
    from_left = around(piece, 1)
    from_right = around(piece, -1)

    own_set = by_harmonic([class_major], [0], LANES // 2)
    starts = [straight + window * ((place + step) % ring) for step in (0, 3, 1, 2)]
    facing_set = by_harmonic(
        [far[:straight], piece, from_left, from_right, far[straight:]],
        jnp.stack([jnp.zeros_like(place)] + starts),
        LANES // 2,
    )
    stacked = [own_set, facing_set]
    table = folded_table(angles)
    score = functools.partial(best_of_groups, stacked=stacked, table=table, shifts=shifts, rows=rows, scale=scale)

    listings = own * list_length
    padded = 16
    listed_shift = shift_ids.reshape(listings)
    listed_image = jnp.arange(listings, dtype=jnp.int32) // list_length
    pick = (listed_shift[:, None, None] == jnp.arange(shifts, dtype=jnp.int32)[None, :, None]) & (
        listed_image[:, None, None] == jnp.arange(own, dtype=jnp.int32)[None, None, :]
    )
    pick = jnp.pad(pick.astype(jnp.bfloat16), ((0, padded - listings), (0, 0), (0, 0)))
    listed = jnp.einsum("lsi,msic->mlc", pick, native, preferred_element_type=jnp.float32).astype(jnp.bfloat16)
    valid = jnp.arange(list_length, dtype=jnp.int32)[None, :] < counts[:, None]
    kept = jnp.where(valid, weights, jnp.zeros_like(weights)).reshape(1, listings)
    flat_ids = class_ids.reshape(1, listings)
    notes = jnp.concatenate(
        [(flat_ids // 16).astype(jnp.bfloat16), (flat_ids % 16).astype(jnp.bfloat16), kept], axis=0
    )
    notes = jnp.pad(notes, ((listings, padded - listings - 3), (0, cycle_parts - listings)))
    payload = (listed + notes[None]).reshape(doms, angles // doms, padded, cycle_parts)
    arrived = lax.all_to_all(payload, "dom", 0, 0, tiled=True)
    noted = arrived[:, 0, listings : listings + 3, :listings]
    ids = noted[:, 0].astype(jnp.int32) * 16 + noted[:, 1].astype(jnp.int32)
    classes = 2 * chips * class_count
    hit = ids[None] == jnp.arange(classes, dtype=jnp.int32)[:, None, None]
    mixing = jnp.where(hit, noted[:, 2][None], jnp.zeros((), jnp.bfloat16))
    totals = jnp.sum(mixing.astype(jnp.float32), axis=(1, 2))
    mixing = jnp.pad(mixing, ((0, 0), (0, 0), (0, padded - listings)))
    sums = jnp.einsum("ksl,smlc->kmc", mixing, arrived, preferred_element_type=jnp.float32)
    depth = angles // doms
    sums = sums.reshape(chips, 2, class_count, depth, cycle_parts)
    totals = jnp.pad(totals.reshape(chips, 2, 1, 1, class_count), ((0, 0), (0, 0), (0, 0), (0, depth - 1), (0, cycle_parts - class_count)))
    sums = jnp.concatenate([sums, totals], axis=2)
    mine = lax.dynamic_index_in_dim(sums, core, 1, keepdims=False)
    other = lax.dynamic_index_in_dim(sums, 1 - core, 1, keepdims=False)
    pair_sums = mine + across(other)
    total = lax.dynamic_index_in_dim(pair_sums, row, 0, keepdims=False)
    for step in range(1, chips):
        block = lax.dynamic_index_in_dim(pair_sums, (row + step) % chips, 0, keepdims=False)
        total = total + along(block, step)
    weight_sums = total[class_count, 0, :class_count]
    class_means = total[:class_count] / jnp.maximum(weight_sums, 1.0)[:, None, None]
    class_means = jnp.transpose(class_means, (1, 0, 2))

    images = [(flat,), (mate,), (lower_partner, upper_partner), (lower_both, upper_both)]
    places = jnp.stack([(row % 2 ^ chip) * 2 + (core ^ other) for chip in range(2) for other in range(2)])
    best = score(places.astype(jnp.int32), images)
    sent = facing(best)
    mine, others = best[:, :class_count], sent[:, LANES // 2 : LANES // 2 + class_count]
    low = jnp.where(row < chips // 2, mine, others)
    high = jnp.where(row < chips // 2, others, mine)
    best_scores = jnp.concatenate([low, high], axis=0)
    return (best_scores, class_means)


def solution(mesh):
    return jax.shard_map(
        on_device,
        mesh=mesh,
        in_specs=(
            P(None, ("dom", "cls"), None, None),
            P(None, "cls", None),
            P(("dom", "cls"), None),
            P(("dom", "cls")),
            P(("dom", "cls"), None),
            P(("dom", "cls"), None),
        ),
        out_specs=(P("dom", "cls"), P("dom", "cls", None)),
        check_vma=False,
    )
```

```python
import functools
import math

import jax
import jax.numpy as jnp
from jax import lax
from jax.experimental import pallas as pl
from jax.experimental.pallas import tpu as pltpu
from jax.sharding import PartitionSpec as P


CHUNK = 16
LANES = 128
WHOLE = pl.BlockSpec(memory_space=pltpu.VMEM)
SCALARS = pl.BlockSpec(memory_space=pltpu.SMEM)


def folded_table(angles):
    half = angles // 2
    index = jnp.arange(half, dtype=jnp.int32)
    product = index[:, None] * index[None, :] % angles
    phase = product.astype(jnp.float32) * (2.0 * math.pi / angles)
    edge = (index[:, None] == 0) | (index[None, :] == 0)
    cosine = jnp.cos(phase)
    sine = jnp.where(edge, 0.0, -jnp.sin(phase))
    alternate = jnp.where(index % 2 == 0, 1.0, -1.0)
    nyquist = jnp.where(index[None, :] == 0, alternate[:, None], 0.0)
    last = jnp.concatenate([alternate, jnp.where(index == 0, 1.0, 0.0)])
    rows = [
        jnp.concatenate([cosine, nyquist], axis=1),
        jnp.concatenate([jnp.zeros_like(sine), sine], axis=1),
        jnp.broadcast_to(last[None, :], (8, angles)),
    ]
    return jnp.concatenate(rows, axis=0).astype(jnp.bfloat16)


def gather_kernel(sizes, starts_ref, *refs):
    pieces, out_ref, work = refs[: len(sizes)], refs[len(sizes)], refs[len(sizes) + 1]
    total = out_ref.shape[1]
    used = sum(map(sum, sizes))
    work[pl.ds(used * CHUNK, (total - used) * CHUNK), :] = jnp.zeros(((total - used) * CHUNK, LANES), jnp.float32)

    def chunk(j, carry):
        base = pl.multiple_of(j * CHUNK, CHUNK)
        k = 0
        for parts, ref in zip(sizes, pieces):
            above = 0
            for size in parts:
                block = ref[above : above + size, pl.ds(base, CHUNK), :].reshape(size * CHUNK, LANES)
                first = pl.multiple_of(starts_ref[k] * CHUNK, CHUNK)
                work[pl.ds(first, size * CHUNK), :] = block.astype(jnp.float32)
                above += size
                k += 1
        for t in range(CHUNK):
            out_ref[base + t] = work[pl.ds(t, total, stride=CHUNK), :].astype(jnp.bfloat16)
        return carry

    lax.fori_loop(0, out_ref.shape[0] // CHUNK, chunk, 0)


def by_harmonic(pieces, sizes, starts, total):
    angles, cycle_parts = pieces[0].shape[1:]
    moved = 2 * angles * cycle_parts * (sum(map(sum, sizes)) + total)
    return pl.pallas_call(
        functools.partial(gather_kernel, sizes),
        in_specs=[SCALARS] + [WHOLE] * len(pieces),
        out_specs=WHOLE,
        out_shape=jax.ShapeDtypeStruct((angles, total, cycle_parts), jnp.bfloat16),
        scratch_shapes=[pltpu.VMEM((total * CHUNK, cycle_parts), jnp.float32)],
        compiler_params=pltpu.CompilerParams(vmem_limit_bytes=14 * 1024 * 1024),
        cost_estimate=pl.CostEstimate(flops=0, bytes_accessed=2 * moved, transcendentals=0),
        name="by_harmonic",
    )(jnp.asarray(starts, jnp.int32), *pieces)


def score_kernel(scale, rows, shifts, counts, places_ref, *refs):
    groups = pieces = counts
    stacked = refs[pieces : pieces + 2]
    table_ref, out_ref, left_ref, fa, fb, folded = refs[pieces + 2 :]
    images = refs[:groups]
    half = table_ref.shape[1] // 2
    all_rows = 2 * rows * groups
    pitch = all_rows + 1
    cycles = LANES // 2
    lane = lax.broadcasted_iota(jnp.int32, (1, LANES), 1)
    sign = jnp.where(lane < cycles, 1.0, -1.0)
    block = CHUNK * rows
    steps = half // CHUNK

    everyone = range(groups)

    def chunk(j, carry):
        back = 2 * half - CHUNK - j * CHUNK
        edge = jnp.where(j == 0, half, 2 * half - CHUNK * j)
        for g in everyone:
            fa[g] = images[g][pl.ds(pl.multiple_of(j * block, block), block), :].astype(jnp.float32)
            back_rows = pl.multiple_of(back * rows, block)
            fb[g, pl.ds(0, block), :] = images[g][pl.ds(back_rows, block), :].astype(jnp.float32)
            edge_rows = pl.multiple_of(edge * rows, block)
            fb[g, pl.ds(block, 2 * rows), :] = images[g][pl.ds(edge_rows, 2 * rows), :].astype(jnp.float32)
        paired = jnp.where(j == 0, 0.0, 1.0)
        for t in range(CHUNK):
            slot = t % left_ref.shape[0]
            for g in range(groups):
                a = fa[g, pl.ds(t * rows, rows), :]
                b = fb[g, pl.ds((CHUNK - t) * rows, rows), :]
                a_turned = pltpu.roll(a, cycles, 1) * sign
                b_turned = pltpu.roll(b, cycles, 1) * (-sign)
                if t == 0:
                    b_turned = b_turned * paired + b * (1.0 - paired)
                    a_turned = a_turned * paired
                    b = b * paired
                top = 2 * rows * g
                left_ref[slot, pl.ds(top, rows), pl.ds(0, LANES)] = a
                left_ref[slot, pl.ds(top, rows), pl.ds(LANES, LANES)] = b
                left_ref[slot, pl.ds(top + rows, rows), pl.ds(0, LANES)] = a_turned
                left_ref[slot, pl.ds(top + rows, rows), pl.ds(LANES, LANES)] = b_turned
            m = j * CHUNK + t
            mirror = edge if t == 0 else 2 * half - m
            right = jnp.concatenate(
                [
                    jnp.concatenate([ref[m] for ref in stacked], axis=0),
                    jnp.concatenate([ref[mirror] for ref in stacked], axis=0),
                ],
                axis=1,
            )
            folded[pl.ds(m * pitch, all_rows), :] = lax.dot_general(
                left_ref[slot].astype(jnp.bfloat16),
                right,
                (((1,), (1,)), ((), ())),
                preferred_element_type=jnp.float32,
            )
        return carry

    lax.fori_loop(0, steps, chunk, 0)
    table = table_ref[...]
    each = rows // shifts
    width = 2 * LANES

    def column(g, n):
        even = folded[pl.ds(2 * rows * g + n, half, stride=pitch), :]
        odd = folded[pl.ds(2 * rows * g + rows + n, half, stride=pitch), :]
        return jnp.concatenate([even, odd], axis=0).astype(jnp.bfloat16)

    def one_shift(s, best):
        better = []
        for q in range(groups * each // 2):
            columns = [column(i // each, s * each + i % each) for i in (2 * q, 2 * q + 1)]
            turned = jnp.dot(table, jnp.concatenate(columns, axis=1), preferred_element_type=jnp.float32)
            both = turned[:half] + jnp.abs(turned[half : 2 * half])
            top = jnp.max(both.reshape(half // 8, 8, width), axis=0)
            top = jnp.maximum(top, turned[2 * half :])
            better.append(jnp.maximum(best[q], top))
        return tuple(better)

    start = tuple(jnp.full((8, width), -jnp.inf, jnp.float32) for _ in range(groups * each // 2))
    best = lax.fori_loop(0, shifts, one_shift, start)
    for q in range(groups * each // 2):
        top = jnp.max(best[q], axis=0, keepdims=True) * scale
        first = places_ref[2 * q // each] * each + 2 * q % each
        out_ref[pl.ds(first, 1), :] = top[:, :LANES]
        out_ref[pl.ds(first + 1, 1), :] = top[:, LANES:]


def best_of_groups(places, images, stacked, table, shifts, rows, scale):
    angles, _, cycle_parts = stacked[0].shape
    half = angles // 2
    each = rows // shifts
    groups = len(images)
    flops = groups * (2 * half * 2 * rows * 2 * cycle_parts * LANES + 2 * rows * LANES * angles * (angles + 8))
    return pl.pallas_call(
        functools.partial(score_kernel, scale, rows, shifts, groups),
        in_specs=[SCALARS] + [WHOLE] * (groups + 3),
        out_specs=WHOLE,
        out_shape=jax.ShapeDtypeStruct((groups * each, LANES), jnp.float32),
        scratch_shapes=[
            pltpu.VMEM((4, 2 * rows * groups, 2 * cycle_parts), jnp.float32),
            pltpu.VMEM((groups, CHUNK * rows, cycle_parts), jnp.float32),
            pltpu.VMEM((groups, (CHUNK + 2) * rows, cycle_parts), jnp.float32),
            pltpu.VMEM(((2 * rows * groups + 1) * half, LANES), jnp.float32),
        ],
        compiler_params=pltpu.CompilerParams(vmem_limit_bytes=36 * 1024 * 1024),
        cost_estimate=pl.CostEstimate(flops=6 * flops, bytes_accessed=20_000_000, transcendentals=0),
        name="score",
    )(places, *images, *stacked, table)


def on_device(particles, references, class_ids, counts, shift_ids, weights):
    cls_index = lax.axis_index("cls")
    core = cls_index % 2
    row = cls_index // 2
    angles, own, shifts, cycle_parts = particles.shape
    class_count = references.shape[1]
    list_length = class_ids.shape[1]
    rows = shifts * own
    doms = 32
    chips = 4
    ring = 4
    scale = 1.0 / math.sqrt(1.0 * cycle_parts * angles)

    def move(value, target):
        pairs = [(2 * y + c, 2 * t + e) for y in range(chips) for c in range(2) for t, e in [target(y, c)]]
        return lax.ppermute(value, "cls", pairs)

    def across(value):
        return move(value, lambda y, c: (y, 1 - c))

    def facing(value):
        return move(value, lambda y, c: (chips - 1 - y, c))

    def around(value, step):
        length = doms // ring
        pairs = [(x * length + z, (x + step) % ring * length + z) for x in range(ring) for z in range(length)]
        return lax.ppermute(value, "dom", pairs)

    native = jnp.transpose(particles, (0, 2, 1, 3))
    flat = native.reshape(angles * rows, cycle_parts)
    class_major = jnp.transpose(references, (1, 0, 2))

    partner = move(flat, lambda y, c: (y ^ 1, c))
    mate = across(flat)
    partner_mate = across(partner)

    place = lax.axis_index("dom") // (doms // ring)
    window = class_count // (ring + 1)
    straight = class_count - ring * window

    def window_of(x):
        return lax.dynamic_slice_in_dim(class_major, straight + window * x, window, 0)

    piece = facing(window_of(place))
    far = facing(jnp.concatenate([class_major[:straight], window_of((place + 2) % ring)]))
    from_left = around(piece, 1)
    from_right = around(piece, -1)

    own_set = by_harmonic([class_major], [(class_count,)], [0], LANES // 2)
    starts = [straight + window * ((place + step) % ring) for step in (2, 0, 3, 1)]
    facing_set = by_harmonic(
        [far, piece, from_left, from_right],
        [(straight, window)] + [(window,)] * 3,
        jnp.stack([jnp.zeros_like(place)] + starts),
        LANES // 2,
    )
    stacked = [own_set, facing_set]
    table = folded_table(angles)
    score = functools.partial(best_of_groups, stacked=stacked, table=table, shifts=shifts, rows=rows, scale=scale)

    listings = own * list_length
    padded = 16
    listed_shift = shift_ids.reshape(listings)
    listed_image = jnp.arange(listings, dtype=jnp.int32) // list_length
    pick = (listed_shift[:, None, None] == jnp.arange(shifts, dtype=jnp.int32)[None, :, None]) & (
        listed_image[:, None, None] == jnp.arange(own, dtype=jnp.int32)[None, None, :]
    )
    pick = jnp.pad(pick.astype(jnp.bfloat16), ((0, padded - listings), (0, 0), (0, 0)))
    listed = jnp.einsum("lsi,msic->mlc", pick, native, preferred_element_type=jnp.float32).astype(jnp.bfloat16)
    valid = jnp.arange(list_length, dtype=jnp.int32)[None, :] < counts[:, None]
    kept = jnp.where(valid, weights, jnp.zeros_like(weights)).reshape(1, listings)
    flat_ids = class_ids.reshape(1, listings)
    notes = jnp.concatenate(
        [(flat_ids // 16).astype(jnp.bfloat16), (flat_ids % 16).astype(jnp.bfloat16), kept], axis=0
    )
    notes = jnp.pad(notes, ((listings, padded - listings - 3), (0, cycle_parts - listings)))
    payload = (listed + notes[None]).reshape(doms, angles // doms, padded, cycle_parts)
    arrived = lax.all_to_all(payload, "dom", 0, 0, tiled=True)
    noted = arrived[:, 0, listings : listings + 3, :listings]
    ids = noted[:, 0].astype(jnp.int32) * 16 + noted[:, 1].astype(jnp.int32)
    classes = 2 * chips * class_count
    hit = ids[None] == jnp.arange(classes, dtype=jnp.int32)[:, None, None]
    mixing = jnp.where(hit, noted[:, 2][None], jnp.zeros((), jnp.bfloat16))
    totals = jnp.sum(mixing.astype(jnp.float32), axis=(1, 2))
    mixing = jnp.pad(mixing, ((0, 0), (0, 0), (0, padded - listings)))
    sums = jnp.einsum("ksl,smlc->kmc", mixing, arrived, preferred_element_type=jnp.float32)
    depth = angles // doms
    sums = sums.reshape(2 * chips, class_count, depth, cycle_parts)
    totals = totals.reshape(2 * chips, 1, 1, class_count)
    totals = jnp.pad(totals, ((0, 0), (0, 0), (0, depth - 1), (0, cycle_parts - class_count)))
    sums = jnp.concatenate([sums, totals], axis=1)
    shares = lax.all_to_all(sums, "cls", 0, 0, tiled=True)
    total = jnp.sum(shares, axis=0)
    weight_sums = total[class_count, 0, :class_count]
    class_means = total[:class_count] / jnp.maximum(weight_sums, 1.0)[:, None, None]
    class_means = jnp.transpose(class_means, (1, 0, 2))

    images = [flat, mate, partner, partner_mate]
    places = jnp.stack([(row % 2 ^ chip) * 2 + (core ^ other) for chip in range(2) for other in range(2)])
    best = score(places.astype(jnp.int32), images)
    sent = facing(best)
    mine, others = best[:, :class_count], sent[:, LANES // 2 : LANES // 2 + class_count]
    low = jnp.where(row < chips // 2, mine, others)
    high = jnp.where(row < chips // 2, others, mine)
    best_scores = jnp.concatenate([low, high], axis=0)
    return (best_scores, class_means)


def solution(mesh):
    return jax.shard_map(
        on_device,
        mesh=mesh,
        in_specs=(
            P(None, ("dom", "cls"), None, None),
            P(None, "cls", None),
            P(("dom", "cls"), None),
            P(("dom", "cls")),
            P(("dom", "cls"), None),
            P(("dom", "cls"), None),
        ),
        out_specs=(P("dom", "cls"), P("dom", "cls", None)),
        check_vma=False,
    )
```

```python
import functools
import math

import jax
import jax.numpy as jnp
from jax import lax
from jax.experimental import pallas as pl
from jax.experimental.pallas import tpu as pltpu
from jax.sharding import PartitionSpec as P


CHUNK = 16
LANES = 128
WHOLE = pl.BlockSpec(memory_space=pltpu.VMEM)
SCALARS = pl.BlockSpec(memory_space=pltpu.SMEM)


def folded_table(angles):
    half = angles // 2
    index = jnp.arange(half, dtype=jnp.int32)
    product = index[:, None] * index[None, :] % angles
    phase = product.astype(jnp.float32) * (2.0 * math.pi / angles)
    edge = (index[:, None] == 0) | (index[None, :] == 0)
    cosine = jnp.cos(phase)
    sine = jnp.where(edge, 0.0, -jnp.sin(phase))
    alternate = jnp.where(index % 2 == 0, 1.0, -1.0)
    nyquist = jnp.where(index[None, :] == 0, alternate[:, None], 0.0)
    last = jnp.concatenate([alternate, jnp.where(index == 0, 1.0, 0.0)])
    rows = [
        jnp.concatenate([cosine, nyquist], axis=1),
        jnp.concatenate([jnp.zeros_like(sine), sine], axis=1),
        jnp.broadcast_to(last[None, :], (8, angles)),
    ]
    return jnp.concatenate(rows, axis=0).astype(jnp.bfloat16)


def gather_kernel(sizes, starts_ref, *refs):
    pieces, out_ref, work = refs[: len(sizes)], refs[len(sizes)], refs[len(sizes) + 1]
    total = out_ref.shape[1]
    used = sum(map(sum, sizes))
    work[pl.ds(used * CHUNK, (total - used) * CHUNK), :] = jnp.zeros(((total - used) * CHUNK, LANES), jnp.float32)

    def chunk(j, carry):
        base = pl.multiple_of(j * CHUNK, CHUNK)
        k = 0
        for parts, ref in zip(sizes, pieces):
            above = 0
            for size in parts:
                block = ref[above : above + size, pl.ds(base, CHUNK), :].reshape(size * CHUNK, LANES)
                first = pl.multiple_of(starts_ref[k] * CHUNK, CHUNK)
                work[pl.ds(first, size * CHUNK), :] = block.astype(jnp.float32)
                above += size
                k += 1
        for t in range(CHUNK):
            out_ref[base + t] = work[pl.ds(t, total, stride=CHUNK), :].astype(jnp.bfloat16)
        return carry

    lax.fori_loop(0, out_ref.shape[0] // CHUNK, chunk, 0)


def by_harmonic(pieces, sizes, starts, total):
    angles, cycle_parts = pieces[0].shape[1:]
    moved = 2 * angles * cycle_parts * (sum(map(sum, sizes)) + total)
    return pl.pallas_call(
        functools.partial(gather_kernel, sizes),
        in_specs=[SCALARS] + [WHOLE] * len(pieces),
        out_specs=WHOLE,
        out_shape=jax.ShapeDtypeStruct((angles, total, cycle_parts), jnp.bfloat16),
        scratch_shapes=[pltpu.VMEM((total * CHUNK, cycle_parts), jnp.float32)],
        compiler_params=pltpu.CompilerParams(vmem_limit_bytes=14 * 1024 * 1024),
        cost_estimate=pl.CostEstimate(flops=0, bytes_accessed=2 * moved, transcendentals=0),
        name="by_harmonic",
    )(jnp.asarray(starts, jnp.int32), *pieces)


def score_kernel(scale, rows, shifts, counts, places_ref, *refs):
    groups = pieces = counts
    stacked = refs[pieces : pieces + 2]
    table_ref, out_ref, left_ref, fa, fb, folded = refs[pieces + 2 :]
    images = refs[:groups]
    half = table_ref.shape[1] // 2
    all_rows = 2 * rows * groups
    pitch = all_rows + 1
    cycles = LANES // 2
    lane = lax.broadcasted_iota(jnp.int32, (1, LANES), 1)
    sign = jnp.where(lane < cycles, 1.0, -1.0)
    block = CHUNK * rows
    steps = half // CHUNK

    everyone = range(groups)

    def chunk(j, carry):
        back = 2 * half - CHUNK - j * CHUNK
        edge = jnp.where(j == 0, half, 2 * half - CHUNK * j)
        for g in everyone:
            fa[g] = images[g][pl.ds(pl.multiple_of(j * block, block), block), :].astype(jnp.float32)
            back_rows = pl.multiple_of(back * rows, block)
            fb[g, pl.ds(0, block), :] = images[g][pl.ds(back_rows, block), :].astype(jnp.float32)
            edge_rows = pl.multiple_of(edge * rows, block)
            fb[g, pl.ds(block, 2 * rows), :] = images[g][pl.ds(edge_rows, 2 * rows), :].astype(jnp.float32)
        paired = jnp.where(j == 0, 0.0, 1.0)
        for t in range(CHUNK):
            slot = t % left_ref.shape[0]
            for g in range(groups):
                a = fa[g, pl.ds(t * rows, rows), :]
                b = fb[g, pl.ds((CHUNK - t) * rows, rows), :]
                a_turned = pltpu.roll(a, cycles, 1) * sign
                b_turned = pltpu.roll(b, cycles, 1) * (-sign)
                if t == 0:
                    b_turned = b_turned * paired + b * (1.0 - paired)
                    a_turned = a_turned * paired
                    b = b * paired
                top = 2 * rows * g
                left_ref[slot, pl.ds(top, rows), pl.ds(0, LANES)] = a
                left_ref[slot, pl.ds(top, rows), pl.ds(LANES, LANES)] = b
                left_ref[slot, pl.ds(top + rows, rows), pl.ds(0, LANES)] = a_turned
                left_ref[slot, pl.ds(top + rows, rows), pl.ds(LANES, LANES)] = b_turned
            m = j * CHUNK + t
            mirror = edge if t == 0 else 2 * half - m
            right = jnp.concatenate(
                [
                    jnp.concatenate([ref[m] for ref in stacked], axis=0),
                    jnp.concatenate([ref[mirror] for ref in stacked], axis=0),
                ],
                axis=1,
            )
            folded[pl.ds(m * pitch, all_rows), :] = lax.dot_general(
                left_ref[slot].astype(jnp.bfloat16),
                right,
                (((1,), (1,)), ((), ())),
                preferred_element_type=jnp.float32,
            )
        return carry

    lax.fori_loop(0, steps, chunk, 0)
    table = table_ref[...]
    each = rows // shifts
    width = 2 * LANES

    def column(g, n):
        even = folded[pl.ds(2 * rows * g + n, half, stride=pitch), :]
        odd = folded[pl.ds(2 * rows * g + rows + n, half, stride=pitch), :]
        return jnp.concatenate([even, odd], axis=0).astype(jnp.bfloat16)

    def one_shift(s, best):
        better = []
        for q in range(groups * each // 2):
            columns = [column(i // each, s * each + i % each) for i in (2 * q, 2 * q + 1)]
            turned = jnp.dot(table, jnp.concatenate(columns, axis=1), preferred_element_type=jnp.float32)
            both = turned[:half] + jnp.abs(turned[half : 2 * half])
            top = jnp.max(both.reshape(half // 8, 8, width), axis=0)
            top = jnp.maximum(top, turned[2 * half :])
            better.append(jnp.maximum(best[q], top))
        return tuple(better)

    start = tuple(jnp.full((8, width), -jnp.inf, jnp.float32) for _ in range(groups * each // 2))
    best = lax.fori_loop(0, shifts, one_shift, start)
    for q in range(groups * each // 2):
        top = jnp.max(best[q], axis=0, keepdims=True) * scale
        first = places_ref[2 * q // each] * each + 2 * q % each
        out_ref[pl.ds(first, 1), :] = top[:, :LANES]
        out_ref[pl.ds(first + 1, 1), :] = top[:, LANES:]


def best_of_groups(places, images, stacked, table, shifts, rows, scale):
    angles, _, cycle_parts = stacked[0].shape
    half = angles // 2
    each = rows // shifts
    groups = len(images)
    flops = groups * (2 * half * 2 * rows * 2 * cycle_parts * LANES + 2 * rows * LANES * angles * (angles + 8))
    return pl.pallas_call(
        functools.partial(score_kernel, scale, rows, shifts, groups),
        in_specs=[SCALARS] + [WHOLE] * (groups + 3),
        out_specs=WHOLE,
        out_shape=jax.ShapeDtypeStruct((groups * each, LANES), jnp.float32),
        scratch_shapes=[
            pltpu.VMEM((4, 2 * rows * groups, 2 * cycle_parts), jnp.float32),
            pltpu.VMEM((groups, CHUNK * rows, cycle_parts), jnp.float32),
            pltpu.VMEM((groups, (CHUNK + 2) * rows, cycle_parts), jnp.float32),
            pltpu.VMEM(((2 * rows * groups + 1) * half, LANES), jnp.float32),
        ],
        compiler_params=pltpu.CompilerParams(vmem_limit_bytes=26 * 1024 * 1024),
        cost_estimate=pl.CostEstimate(flops=6 * flops, bytes_accessed=20_000_000, transcendentals=0),
        name="score",
    )(places, *images, *stacked, table)


def listing_kernel(shift_ref, id_ref, count_ref, weight_ref, images_ref, out_ref, work):
    own, length = id_ref.shape
    owners, tiles, depth, cycle_parts = out_ref.shape
    angles = owners * depth
    rows = images_ref.shape[0] // angles
    block = CHUNK * rows

    def widen(j, carry):
        part = pl.ds(pl.multiple_of(j * block, block), block)
        work[part, :] = images_ref[part, :].astype(jnp.float32)
        return carry

    lax.fori_loop(0, angles // CHUNK, widen, 0)
    lane = lax.broadcasted_iota(jnp.int32, (depth, cycle_parts), 1)
    digit = lax.broadcasted_iota(jnp.int32, (depth, cycle_parts), 0)
    notes = jnp.zeros((depth, cycle_parts), jnp.float32)
    for i in range(own):
        for j in range(length):
            place = i * length + j
            column = work[pl.ds(shift_ref[i, j] * own + i, angles, stride=rows), :]
            out_ref[:, place] = column.reshape(owners, depth, cycle_parts).astype(jnp.bfloat16)
            name = id_ref[i, j]
            kept = jnp.where(j < count_ref[i], weight_ref[i, j], 0.0)
            upper = (name >> 4).astype(jnp.float32)
            lower = (name & 15).astype(jnp.float32)
            value = jnp.where(digit == 0, upper, jnp.where(digit == 1, lower, jnp.where(digit == 2, kept, 0.0)))
            notes = jnp.where(lane == place, value, notes)
    out_ref[:, tiles - 1] = jnp.broadcast_to(notes.astype(jnp.bfloat16)[None], (owners, depth, cycle_parts))


def listings_by_owner(shift_ids, class_ids, counts, weights, images, owners):
    own, length = class_ids.shape
    cycle_parts = images.shape[1]
    rows = images.shape[0]
    angles = rows // (9 * own)
    shape = (owners, own * length + 1, angles // owners, cycle_parts)
    return pl.pallas_call(
        listing_kernel,
        in_specs=[SCALARS] * 4 + [WHOLE],
        out_specs=WHOLE,
        out_shape=jax.ShapeDtypeStruct(shape, jnp.bfloat16),
        scratch_shapes=[pltpu.VMEM((rows, cycle_parts), jnp.float32)],
        compiler_params=pltpu.CompilerParams(vmem_limit_bytes=14 * 1024 * 1024),
        cost_estimate=pl.CostEstimate(flops=0, bytes_accessed=8_000_000, transcendentals=0),
        name="listings",
    )(shift_ids, class_ids, counts, weights, images)


def sums_kernel(class_count, sets, arrived_ref, out_ref, work):
    sources, tiles, depth, cycle_parts = arrived_ref.shape
    listings = tiles - 1
    each = tiles * depth
    places = work.shape[0] // depth
    used = sources * each
    padded = -(-class_count // 8) * 8

    def widen(j, carry):
        first = pl.multiple_of(j * each, each)
        work[pl.ds(first, each), :] = arrived_ref[j].reshape(each, cycle_parts).astype(jnp.float32)
        return carry

    lax.fori_loop(0, sources, widen, 0)
    work[pl.ds(used, work.shape[0] - used), :] = jnp.zeros((work.shape[0] - used, cycle_parts), jnp.float32)
    lane = lax.broadcasted_iota(jnp.int32, (1, LANES), 1)
    names = [jnp.zeros((1, LANES), jnp.float32) for _ in range(places // LANES)]
    kept = [jnp.zeros((1, LANES), jnp.float32) for _ in range(places // LANES)]
    for source in range(sources):
        first = source * each + listings * depth
        name = work[pl.ds(first, 1), :] * 16.0 + work[pl.ds(first + 1, 1), :]
        weight = work[pl.ds(first + 2, 1), :]
        column, offset = divmod(source * tiles, LANES)
        if offset:
            name, weight = pltpu.roll(name, offset, 1), pltpu.roll(weight, offset, 1)
        here = lane >= offset
        names[column] = names[column] + jnp.where(here, name, 0.0)
        kept[column] = kept[column] + jnp.where(here, weight, 0.0)
        if offset + listings > LANES:
            names[column + 1] = names[column + 1] + jnp.where(here, 0.0, name)
            kept[column + 1] = kept[column + 1] + jnp.where(here, 0.0, weight)
    names = jnp.concatenate(names, axis=1)
    kept = jnp.concatenate(kept, axis=1)

    def mixing_of(block, rows):
        row = lax.broadcasted_iota(jnp.int32, (rows, places), 0)
        wanted = (row + block * class_count).astype(jnp.float32)
        return jnp.where((wanted == names) & (row < class_count), kept, 0.0).astype(jnp.bfloat16)

    mixing = jnp.concatenate([mixing_of(block, padded) for block in range(sets)], axis=0)
    ones = jnp.ones((8, places), jnp.bfloat16)
    for block in range(sets):
        total = lax.dot_general(
            ones, mixing_of(block, LANES), (((1,), (1,)), ((), ())), preferred_element_type=jnp.float32
        )
        out_ref[pl.ds((block * (class_count + 1) + class_count) * depth, depth), :] = total
    for m in range(0, depth, 2):
        pair = [work[pl.ds(m + k, places, stride=depth), :].astype(jnp.bfloat16) for k in range(2)]
        result = jnp.dot(mixing, jnp.concatenate(pair, axis=1), preferred_element_type=jnp.float32)
        for k in range(2):
            for block in range(sets):
                for first in range(0, class_count, 8):
                    n = min(8, class_count - first)
                    start = (block * (class_count + 1) + first) * depth + m + k
                    row = block * padded + first
                    out_ref[pl.ds(start, n, stride=depth), :] = result[
                        row : row + n, k * cycle_parts : (k + 1) * cycle_parts
                    ]


def class_shares(arrived, class_count, sets):
    sources, tiles, depth, cycle_parts = arrived.shape
    places = -(-sources * tiles // LANES) * LANES
    rows = sets * (class_count + 1) * depth
    return pl.pallas_call(
        functools.partial(sums_kernel, class_count, sets),
        in_specs=[WHOLE],
        out_specs=WHOLE,
        out_shape=jax.ShapeDtypeStruct((rows, cycle_parts), jnp.float32),
        scratch_shapes=[pltpu.VMEM((places * depth, cycle_parts), jnp.float32)],
        compiler_params=pltpu.CompilerParams(vmem_limit_bytes=14 * 1024 * 1024),
        cost_estimate=pl.CostEstimate(flops=4_000_000_000, bytes_accessed=8_000_000, transcendentals=0),
        name="shares",
    )(arrived)


def on_device(particles, references, class_ids, counts, shift_ids, weights):
    cls_index = lax.axis_index("cls")
    core = cls_index % 2
    row = cls_index // 2
    angles, own, shifts, cycle_parts = particles.shape
    class_count = references.shape[1]
    rows = shifts * own
    doms = 32
    chips = 4
    ring = 4
    scale = 1.0 / math.sqrt(1.0 * cycle_parts * angles)

    def move(value, target):
        pairs = [(2 * y + c, 2 * t + e) for y in range(chips) for c in range(2) for t, e in [target(y, c)]]
        return lax.ppermute(value, "cls", pairs)

    def across(value):
        return move(value, lambda y, c: (y, 1 - c))

    def facing(value):
        return move(value, lambda y, c: (chips - 1 - y, c))

    def around(value, step):
        length = doms // ring
        pairs = [(x * length + z, (x + step) % ring * length + z) for x in range(ring) for z in range(length)]
        return lax.ppermute(value, "dom", pairs)

    native = jnp.transpose(particles, (0, 2, 1, 3))
    flat = native.reshape(angles * rows, cycle_parts)
    class_major = jnp.transpose(references, (1, 0, 2))

    partner = move(flat, lambda y, c: (y ^ 1, c))
    mate = across(flat)
    partner_mate = across(partner)

    place = lax.axis_index("dom") // (doms // ring)
    window = class_count // (ring + 1)
    straight = class_count - ring * window

    def window_of(x):
        return lax.dynamic_slice_in_dim(class_major, straight + window * x, window, 0)

    piece = facing(window_of(place))
    far = facing(jnp.concatenate([class_major[:straight], window_of((place + 2) % ring)]))
    from_left = around(piece, 1)
    from_right = around(piece, -1)

    own_set = by_harmonic([class_major], [(class_count,)], [0], LANES // 2)
    starts = [straight + window * ((place + step) % ring) for step in (2, 0, 3, 1)]
    facing_set = by_harmonic(
        [far, piece, from_left, from_right],
        [(straight, window)] + [(window,)] * 3,
        jnp.stack([jnp.zeros_like(place)] + starts),
        LANES // 2,
    )
    stacked = [own_set, facing_set]
    table = folded_table(angles)
    score = functools.partial(best_of_groups, stacked=stacked, table=table, shifts=shifts, rows=rows, scale=scale)

    depth = angles // doms
    payload = listings_by_owner(shift_ids, class_ids, counts, weights.astype(jnp.float32), flat, doms)
    tiles = payload.shape[1]
    arrived = lax.all_to_all(payload.reshape(doms, tiles * depth, cycle_parts), "dom", 0, 0, tiled=True)
    sums = class_shares(arrived.reshape(doms, tiles, depth, cycle_parts), class_count, 2 * chips)
    sums = sums.reshape(2 * chips, class_count + 1, depth, cycle_parts)
    shares = lax.all_to_all(sums, "cls", 0, 0, tiled=True)
    total = jnp.sum(shares, axis=0)
    weight_sums = total[class_count, 0, :class_count]
    class_means = total[:class_count] / jnp.maximum(weight_sums, 1.0)[:, None, None]
    class_means = jnp.transpose(class_means, (1, 0, 2))

    images = [flat, mate, partner, partner_mate]
    places = jnp.stack([(row % 2 ^ chip) * 2 + (core ^ other) for chip in range(2) for other in range(2)])
    places = places.astype(jnp.int32)
    home = score(places[:2] % 2, images[:2])
    away = score(places[2:] % 2, images[2:])
    even = row % 2 == 0
    best = jnp.concatenate([jnp.where(even, home, away), jnp.where(even, away, home)], axis=0)
    sent = facing(best)
    mine, others = best[:, :class_count], sent[:, LANES // 2 : LANES // 2 + class_count]
    low = jnp.where(row < chips // 2, mine, others)
    high = jnp.where(row < chips // 2, others, mine)
    best_scores = jnp.concatenate([low, high], axis=0)
    return (best_scores, class_means)


def solution(mesh):
    return jax.shard_map(
        on_device,
        mesh=mesh,
        in_specs=(
            P(None, ("dom", "cls"), None, None),
            P(None, "cls", None),
            P(("dom", "cls"), None),
            P(("dom", "cls")),
            P(("dom", "cls"), None),
            P(("dom", "cls"), None),
        ),
        out_specs=(P("dom", "cls"), P("dom", "cls", None)),
        check_vma=False,
    )
```

```python
import functools
import math

import jax
import jax.numpy as jnp
from jax import lax
from jax.experimental import pallas as pl
from jax.experimental.pallas import tpu as pltpu
from jax.sharding import PartitionSpec as P


CHUNK = 16
LANES = 128
WHOLE = pl.BlockSpec(memory_space=pltpu.VMEM)
SCALARS = pl.BlockSpec(memory_space=pltpu.SMEM)


def folded_table(angles):
    half = angles // 2
    index = jnp.arange(half, dtype=jnp.int32)
    product = index[:, None] * index[None, :] % angles
    phase = product.astype(jnp.float32) * (2.0 * math.pi / angles)
    edge = (index[:, None] == 0) | (index[None, :] == 0)
    cosine = jnp.cos(phase)
    sine = jnp.where(edge, 0.0, -jnp.sin(phase))
    alternate = jnp.where(index % 2 == 0, 1.0, -1.0)
    nyquist = jnp.where(index[None, :] == 0, alternate[:, None], 0.0)
    last = jnp.concatenate([alternate, jnp.where(index == 0, 1.0, 0.0)])
    rows = [
        jnp.concatenate([cosine, nyquist], axis=1),
        jnp.concatenate([jnp.zeros_like(sine), sine], axis=1),
        jnp.broadcast_to(last[None, :], (8, angles)),
    ]
    return jnp.concatenate(rows, axis=0).astype(jnp.bfloat16)


def gather_kernel(sizes, starts_ref, *refs):
    pieces, out_ref, work = refs[: len(sizes)], refs[len(sizes)], refs[len(sizes) + 1]
    total = out_ref.shape[1]
    used = sum(map(sum, sizes))
    work[pl.ds(used * CHUNK, (total - used) * CHUNK), :] = jnp.zeros(((total - used) * CHUNK, LANES), jnp.float32)

    def chunk(j, carry):
        base = pl.multiple_of(j * CHUNK, CHUNK)
        k = 0
        for parts, ref in zip(sizes, pieces):
            above = 0
            for size in parts:
                block = ref[above : above + size, pl.ds(base, CHUNK), :].reshape(size * CHUNK, LANES)
                first = pl.multiple_of(starts_ref[k] * CHUNK, CHUNK)
                work[pl.ds(first, size * CHUNK), :] = block.astype(jnp.float32)
                above += size
                k += 1
        for t in range(CHUNK):
            out_ref[base + t] = work[pl.ds(t, total, stride=CHUNK), :].astype(jnp.bfloat16)
        return carry

    lax.fori_loop(0, out_ref.shape[0] // CHUNK, chunk, 0)


def by_harmonic(pieces, sizes, starts, total):
    angles, cycle_parts = pieces[0].shape[1:]
    moved = 2 * angles * cycle_parts * (sum(map(sum, sizes)) + total)
    return pl.pallas_call(
        functools.partial(gather_kernel, sizes),
        in_specs=[SCALARS] + [WHOLE] * len(pieces),
        out_specs=WHOLE,
        out_shape=jax.ShapeDtypeStruct((angles, total, cycle_parts), jnp.bfloat16),
        scratch_shapes=[pltpu.VMEM((total * CHUNK, cycle_parts), jnp.float32)],
        compiler_params=pltpu.CompilerParams(vmem_limit_bytes=14 * 1024 * 1024),
        cost_estimate=pl.CostEstimate(flops=0, bytes_accessed=2 * moved, transcendentals=0),
        name="by_harmonic",
    )(jnp.asarray(starts, jnp.int32), *pieces)


def score_kernel(scale, rows, shifts, counts, places_ref, *refs):
    groups = pieces = counts
    stacked = refs[pieces : pieces + 2]
    table_ref, out_ref, left_ref, fa, fb, folded = refs[pieces + 2 :]
    images = refs[:groups]
    half = table_ref.shape[1] // 2
    all_rows = 2 * rows * groups
    pitch = all_rows + 1
    cycles = LANES // 2
    lane = lax.broadcasted_iota(jnp.int32, (1, LANES), 1)
    sign = jnp.where(lane < cycles, 1.0, -1.0)
    block = CHUNK * rows
    steps = half // CHUNK

    everyone = range(groups)

    def chunk(j, carry):
        back = 2 * half - CHUNK - j * CHUNK
        edge = jnp.where(j == 0, half, 2 * half - CHUNK * j)
        for g in everyone:
            fa[g] = images[g][pl.ds(pl.multiple_of(j * block, block), block), :].astype(jnp.float32)
            back_rows = pl.multiple_of(back * rows, block)
            fb[g, pl.ds(0, block), :] = images[g][pl.ds(back_rows, block), :].astype(jnp.float32)
            edge_rows = pl.multiple_of(edge * rows, block)
            fb[g, pl.ds(block, 2 * rows), :] = images[g][pl.ds(edge_rows, 2 * rows), :].astype(jnp.float32)
        paired = jnp.where(j == 0, 0.0, 1.0)
        for t in range(CHUNK):
            slot = t % left_ref.shape[0]
            for g in range(groups):
                a = fa[g, pl.ds(t * rows, rows), :]
                b = fb[g, pl.ds((CHUNK - t) * rows, rows), :]
                a_turned = pltpu.roll(a, cycles, 1) * sign
                b_turned = pltpu.roll(b, cycles, 1) * (-sign)
                if t == 0:
                    b_turned = b_turned * paired + b * (1.0 - paired)
                    a_turned = a_turned * paired
                    b = b * paired
                top = 2 * rows * g
                left_ref[slot, pl.ds(top, rows), pl.ds(0, LANES)] = a
                left_ref[slot, pl.ds(top, rows), pl.ds(LANES, LANES)] = b
                left_ref[slot, pl.ds(top + rows, rows), pl.ds(0, LANES)] = a_turned
                left_ref[slot, pl.ds(top + rows, rows), pl.ds(LANES, LANES)] = b_turned
            m = j * CHUNK + t
            mirror = edge if t == 0 else 2 * half - m
            right = jnp.concatenate(
                [
                    jnp.concatenate([ref[m] for ref in stacked], axis=0),
                    jnp.concatenate([ref[mirror] for ref in stacked], axis=0),
                ],
                axis=1,
            )
            folded[pl.ds(m * pitch, all_rows), :] = lax.dot_general(
                left_ref[slot].astype(jnp.bfloat16),
                right,
                (((1,), (1,)), ((), ())),
                preferred_element_type=jnp.float32,
            )
        return carry

    lax.fori_loop(0, steps, chunk, 0)
    table = table_ref[...]
    each = rows // shifts
    width = 2 * LANES

    def column(g, n):
        even = folded[pl.ds(2 * rows * g + n, half, stride=pitch), :]
        odd = folded[pl.ds(2 * rows * g + rows + n, half, stride=pitch), :]
        return jnp.concatenate([even, odd], axis=0).astype(jnp.bfloat16)

    def one_shift(s, best):
        better = []
        for q in range(groups * each // 2):
            columns = [column(i // each, s * each + i % each) for i in (2 * q, 2 * q + 1)]
            turned = jnp.dot(table, jnp.concatenate(columns, axis=1), preferred_element_type=jnp.float32)
            both = turned[:half] + jnp.abs(turned[half : 2 * half])
            top = jnp.max(both.reshape(half // 8, 8, width), axis=0)
            top = jnp.maximum(top, turned[2 * half :])
            better.append(jnp.maximum(best[q], top))
        return tuple(better)

    start = tuple(jnp.full((8, width), -jnp.inf, jnp.float32) for _ in range(groups * each // 2))
    best = lax.fori_loop(0, shifts, one_shift, start)
    for q in range(groups * each // 2):
        top = jnp.max(best[q], axis=0, keepdims=True) * scale
        first = places_ref[2 * q // each] * each + 2 * q % each
        out_ref[pl.ds(first, 1), :] = top[:, :LANES]
        out_ref[pl.ds(first + 1, 1), :] = top[:, LANES:]


def best_of_groups(places, images, stacked, table, shifts, rows, scale):
    angles, _, cycle_parts = stacked[0].shape
    half = angles // 2
    each = rows // shifts
    groups = len(images)
    flops = groups * (2 * half * 2 * rows * 2 * cycle_parts * LANES + 2 * rows * LANES * angles * (angles + 8))
    return pl.pallas_call(
        functools.partial(score_kernel, scale, rows, shifts, groups),
        in_specs=[SCALARS] + [WHOLE] * (groups + 3),
        out_specs=WHOLE,
        out_shape=jax.ShapeDtypeStruct((groups * each, LANES), jnp.float32),
        scratch_shapes=[
            pltpu.VMEM((4, 2 * rows * groups, 2 * cycle_parts), jnp.float32),
            pltpu.VMEM((groups, CHUNK * rows, cycle_parts), jnp.float32),
            pltpu.VMEM((groups, (CHUNK + 2) * rows, cycle_parts), jnp.float32),
            pltpu.VMEM(((2 * rows * groups + 1) * half, LANES), jnp.float32),
        ],
        compiler_params=pltpu.CompilerParams(vmem_limit_bytes=26 * 1024 * 1024),
        cost_estimate=pl.CostEstimate(flops=6 * flops, bytes_accessed=20_000_000, transcendentals=0),
        name="score",
    )(places, *images, *stacked, table)


def listing_kernel(shift_ref, id_ref, count_ref, weight_ref, images_ref, out_ref, work):
    own, length = id_ref.shape
    owners, tiles, depth, cycle_parts = out_ref.shape
    angles = owners * depth
    rows = images_ref.shape[0] // angles
    block = CHUNK * rows

    def widen(j, carry):
        part = pl.ds(pl.multiple_of(j * block, block), block)
        work[part, :] = images_ref[part, :].astype(jnp.float32)
        return carry

    lax.fori_loop(0, angles // CHUNK, widen, 0)
    lane = lax.broadcasted_iota(jnp.int32, (depth, cycle_parts), 1)
    digit = lax.broadcasted_iota(jnp.int32, (depth, cycle_parts), 0)
    notes = jnp.zeros((depth, cycle_parts), jnp.float32)
    for i in range(own):
        for j in range(length):
            place = i * length + j
            column = work[pl.ds(shift_ref[i, j] * own + i, angles, stride=rows), :]
            out_ref[:, place] = column.reshape(owners, depth, cycle_parts).astype(jnp.bfloat16)
            name = id_ref[i, j]
            kept = jnp.where(j < count_ref[i], weight_ref[i, j], 0.0)
            upper = (name >> 4).astype(jnp.float32)
            lower = (name & 15).astype(jnp.float32)
            value = jnp.where(digit == 0, upper, jnp.where(digit == 1, lower, jnp.where(digit == 2, kept, 0.0)))
            notes = jnp.where(lane == place, value, notes)
    out_ref[:, tiles - 1] = jnp.broadcast_to(notes.astype(jnp.bfloat16)[None], (owners, depth, cycle_parts))


def listings_by_owner(shift_ids, class_ids, counts, weights, images, owners):
    own, length = class_ids.shape
    cycle_parts = images.shape[1]
    rows = images.shape[0]
    angles = rows // (9 * own)
    shape = (owners, own * length + 1, angles // owners, cycle_parts)
    return pl.pallas_call(
        listing_kernel,
        in_specs=[SCALARS] * 4 + [WHOLE],
        out_specs=WHOLE,
        out_shape=jax.ShapeDtypeStruct(shape, jnp.bfloat16),
        scratch_shapes=[pltpu.VMEM((rows, cycle_parts), jnp.float32)],
        compiler_params=pltpu.CompilerParams(vmem_limit_bytes=14 * 1024 * 1024),
        cost_estimate=pl.CostEstimate(flops=0, bytes_accessed=8_000_000, transcendentals=0),
        name="listings",
    )(shift_ids, class_ids, counts, weights, images)


def sums_kernel(class_count, sets, arrived_ref, out_ref, work):
    sources, tiles, depth, cycle_parts = arrived_ref.shape
    listings = tiles - 1
    each = tiles * depth
    places = work.shape[0] // depth
    used = sources * each
    padded = -(-class_count // 8) * 8

    def widen(j, carry):
        first = pl.multiple_of(j * each, each)
        work[pl.ds(first, each), :] = arrived_ref[j].reshape(each, cycle_parts).astype(jnp.float32)
        return carry

    lax.fori_loop(0, sources, widen, 0)
    work[pl.ds(used, work.shape[0] - used), :] = jnp.zeros((work.shape[0] - used, cycle_parts), jnp.float32)
    lane = lax.broadcasted_iota(jnp.int32, (1, LANES), 1)
    names = [jnp.zeros((1, LANES), jnp.float32) for _ in range(places // LANES)]
    kept = [jnp.zeros((1, LANES), jnp.float32) for _ in range(places // LANES)]
    for source in range(sources):
        first = source * each + listings * depth
        name = work[pl.ds(first, 1), :] * 16.0 + work[pl.ds(first + 1, 1), :]
        weight = work[pl.ds(first + 2, 1), :]
        column, offset = divmod(source * tiles, LANES)
        if offset:
            name, weight = pltpu.roll(name, offset, 1), pltpu.roll(weight, offset, 1)
        here = lane >= offset
        names[column] = names[column] + jnp.where(here, name, 0.0)
        kept[column] = kept[column] + jnp.where(here, weight, 0.0)
        if offset + listings > LANES:
            names[column + 1] = names[column + 1] + jnp.where(here, 0.0, name)
            kept[column + 1] = kept[column + 1] + jnp.where(here, 0.0, weight)
    names = jnp.concatenate(names, axis=1)
    kept = jnp.concatenate(kept, axis=1)

    def mixing_of(block, rows):
        row = lax.broadcasted_iota(jnp.int32, (rows, places), 0)
        wanted = (row + block * class_count).astype(jnp.float32)
        return jnp.where((wanted == names) & (row < class_count), kept, 0.0).astype(jnp.bfloat16)

    mixing = jnp.concatenate([mixing_of(block, padded) for block in range(sets)], axis=0)
    ones = jnp.ones((8, places), jnp.bfloat16)
    for block in range(sets):
        total = lax.dot_general(
            ones, mixing_of(block, LANES), (((1,), (1,)), ((), ())), preferred_element_type=jnp.float32
        )
        out_ref[pl.ds((block * (class_count + 1) + class_count) * depth, depth), :] = total
    for m in range(0, depth, 2):
        pair = [work[pl.ds(m + k, places, stride=depth), :].astype(jnp.bfloat16) for k in range(2)]
        result = jnp.dot(mixing, jnp.concatenate(pair, axis=1), preferred_element_type=jnp.float32)
        for k in range(2):
            for block in range(sets):
                for first in range(0, class_count, 8):
                    n = min(8, class_count - first)
                    start = (block * (class_count + 1) + first) * depth + m + k
                    row = block * padded + first
                    out_ref[pl.ds(start, n, stride=depth), :] = result[
                        row : row + n, k * cycle_parts : (k + 1) * cycle_parts
                    ]


def class_shares(arrived, class_count, sets):
    sources, tiles, depth, cycle_parts = arrived.shape
    places = -(-sources * tiles // LANES) * LANES
    rows = sets * (class_count + 1) * depth
    return pl.pallas_call(
        functools.partial(sums_kernel, class_count, sets),
        in_specs=[WHOLE],
        out_specs=WHOLE,
        out_shape=jax.ShapeDtypeStruct((rows, cycle_parts), jnp.float32),
        scratch_shapes=[pltpu.VMEM((places * depth, cycle_parts), jnp.float32)],
        compiler_params=pltpu.CompilerParams(vmem_limit_bytes=14 * 1024 * 1024),
        cost_estimate=pl.CostEstimate(flops=4_000_000_000, bytes_accessed=8_000_000, transcendentals=0),
        name="shares",
    )(arrived)


def on_device(particles, references, class_ids, counts, shift_ids, weights):
    cls_index = lax.axis_index("cls")
    core = cls_index % 2
    row = cls_index // 2
    angles, own, shifts, cycle_parts = particles.shape
    class_count = references.shape[1]
    rows = shifts * own
    doms = 32
    chips = 4
    ring = 4
    scale = 1.0 / math.sqrt(1.0 * cycle_parts * angles)

    def move(value, target):
        pairs = [(2 * y + c, 2 * t + e) for y in range(chips) for c in range(2) for t, e in [target(y, c)]]
        return lax.ppermute(value, "cls", pairs)

    def across(value):
        return move(value, lambda y, c: (y, 1 - c))

    def facing(value):
        return move(value, lambda y, c: (chips - 1 - y, c))

    def around(value, step):
        length = doms // ring
        pairs = [(x * length + z, (x + step) % ring * length + z) for x in range(ring) for z in range(length)]
        return lax.ppermute(value, "dom", pairs)

    native = jnp.transpose(particles, (0, 2, 1, 3))
    flat = native.reshape(angles * rows, cycle_parts)
    class_major = jnp.transpose(references, (1, 0, 2))

    partner = move(flat, lambda y, c: (y ^ 1, c))
    mate = across(flat)
    partner_mate = across(partner)

    place = lax.axis_index("dom") // (doms // ring)
    window = class_count // ring
    straight = class_count - ring * window

    def window_of(classes, x):
        return lax.dynamic_slice_in_dim(classes, straight + window * x, window, 0)

    nearest, again = lax.optimization_barrier((window_of(class_major, place), class_major))
    piece = facing(nearest)
    far = facing(jnp.concatenate([again[:straight], window_of(again, (place + 2) % ring)]))
    from_left = around(piece, 1)
    from_right = around(piece, -1)

    own_set = by_harmonic([class_major], [(class_count,)], [0], LANES // 2)
    starts = [straight + window * ((place + step) % ring) for step in (2, 0, 3, 1)]
    facing_set = by_harmonic(
        [far, piece, from_left, from_right],
        [(straight, window)] + [(window,)] * 3,
        jnp.stack([jnp.zeros_like(place)] + starts),
        LANES // 2,
    )
    stacked = [own_set, facing_set]
    table = folded_table(angles)
    score = functools.partial(best_of_groups, stacked=stacked, table=table, shifts=shifts, rows=rows, scale=scale)

    depth = angles // doms
    payload = listings_by_owner(shift_ids, class_ids, counts, weights.astype(jnp.float32), flat, doms)
    tiles = payload.shape[1]
    arrived = lax.all_to_all(payload.reshape(doms, tiles * depth, cycle_parts), "dom", 0, 0, tiled=True)
    sums = class_shares(arrived.reshape(doms, tiles, depth, cycle_parts), class_count, 2 * chips)
    sums = sums.reshape(2 * chips, class_count + 1, depth, cycle_parts)
    shares = lax.all_to_all(sums, "cls", 0, 0, tiled=True)
    total = jnp.sum(shares, axis=0)
    weight_sums = total[class_count, 0, :class_count]
    class_means = total[:class_count] / jnp.maximum(weight_sums, 1.0)[:, None, None]
    class_means = jnp.transpose(class_means, (1, 0, 2))

    images = [flat, mate, partner, partner_mate]
    places = jnp.stack([(row % 2 ^ chip) * 2 + (core ^ other) for chip in range(2) for other in range(2)])
    places = places.astype(jnp.int32)
    home = score(places[:2] % 2, images[:2])
    away = score(places[2:] % 2, images[2:])
    even = row % 2 == 0
    best = jnp.concatenate([jnp.where(even, home, away), jnp.where(even, away, home)], axis=0)
    sent = facing(best)
    mine, others = best[:, :class_count], sent[:, LANES // 2 : LANES // 2 + class_count]
    low = jnp.where(row < chips // 2, mine, others)
    high = jnp.where(row < chips // 2, others, mine)
    best_scores = jnp.concatenate([low, high], axis=0)
    return (best_scores, class_means)


def solution(mesh):
    return jax.shard_map(
        on_device,
        mesh=mesh,
        in_specs=(
            P(None, ("dom", "cls"), None, None),
            P(None, "cls", None),
            P(("dom", "cls"), None),
            P(("dom", "cls")),
            P(("dom", "cls"), None),
            P(("dom", "cls"), None),
        ),
        out_specs=(P("dom", "cls"), P("dom", "cls", None)),
        check_vma=False,
    )
```

```python
import functools
import math

import jax
import jax.numpy as jnp
from jax import lax
from jax.experimental import pallas as pl
from jax.experimental.pallas import tpu as pltpu
from jax.sharding import PartitionSpec as P


CHUNK = 16
LANES = 128
WHOLE = pl.BlockSpec(memory_space=pltpu.VMEM)
SCALARS = pl.BlockSpec(memory_space=pltpu.SMEM)


def folded_table(angles):
    half = angles // 2
    index = jnp.arange(half, dtype=jnp.int32)
    product = index[:, None] * index[None, :] % angles
    phase = product.astype(jnp.float32) * (2.0 * math.pi / angles)
    edge = (index[:, None] == 0) | (index[None, :] == 0)
    cosine = jnp.cos(phase)
    sine = jnp.where(edge, 0.0, -jnp.sin(phase))
    alternate = jnp.where(index % 2 == 0, 1.0, -1.0)
    nyquist = jnp.where(index[None, :] == 0, alternate[:, None], 0.0)
    last = jnp.concatenate([alternate, jnp.where(index == 0, 1.0, 0.0)])
    rows = [
        jnp.concatenate([cosine, nyquist], axis=1),
        jnp.concatenate([jnp.zeros_like(sine), sine], axis=1),
        jnp.broadcast_to(last[None, :], (8, angles)),
    ]
    return jnp.concatenate(rows, axis=0).astype(jnp.bfloat16)


def gather_kernel(sizes, starts_ref, *refs):
    pieces, out_ref, work = refs[: len(sizes)], refs[len(sizes)], refs[len(sizes) + 1]
    total = out_ref.shape[1]
    used = sum(map(sum, sizes))
    work[pl.ds(used * CHUNK, (total - used) * CHUNK), :] = jnp.zeros(((total - used) * CHUNK, LANES), jnp.float32)

    def chunk(j, carry):
        base = pl.multiple_of(j * CHUNK, CHUNK)
        k = 0
        for parts, ref in zip(sizes, pieces):
            above = 0
            for size in parts:
                block = ref[above : above + size, pl.ds(base, CHUNK), :].reshape(size * CHUNK, LANES)
                first = pl.multiple_of(starts_ref[k] * CHUNK, CHUNK)
                work[pl.ds(first, size * CHUNK), :] = block.astype(jnp.float32)
                above += size
                k += 1
        for t in range(CHUNK):
            out_ref[base + t] = work[pl.ds(t, total, stride=CHUNK), :].astype(jnp.bfloat16)
        return carry

    lax.fori_loop(0, out_ref.shape[0] // CHUNK, chunk, 0)


def by_harmonic(pieces, sizes, starts, total):
    angles, cycle_parts = pieces[0].shape[1:]
    moved = 2 * angles * cycle_parts * (sum(map(sum, sizes)) + total)
    return pl.pallas_call(
        functools.partial(gather_kernel, sizes),
        in_specs=[SCALARS] + [WHOLE] * len(pieces),
        out_specs=WHOLE,
        out_shape=jax.ShapeDtypeStruct((angles, total, cycle_parts), jnp.bfloat16),
        scratch_shapes=[pltpu.VMEM((total * CHUNK, cycle_parts), jnp.float32)],
        compiler_params=pltpu.CompilerParams(vmem_limit_bytes=14 * 1024 * 1024),
        cost_estimate=pl.CostEstimate(flops=0, bytes_accessed=2 * moved, transcendentals=0),
        name="by_harmonic",
    )(jnp.asarray(starts, jnp.int32), *pieces)


def score_kernel(scale, rows, shifts, counts, places_ref, *refs):
    groups = pieces = counts
    stacked = refs[pieces : pieces + 2]
    table_ref, out_ref, left_ref, fa, fb, folded = refs[pieces + 2 :]
    images = refs[:groups]
    half = table_ref.shape[1] // 2
    all_rows = 2 * rows * groups
    pitch = all_rows + 1
    cycles = LANES // 2
    lane = lax.broadcasted_iota(jnp.int32, (1, LANES), 1)
    sign = jnp.where(lane < cycles, 1.0, -1.0)
    block = CHUNK * rows
    steps = half // CHUNK

    everyone = range(groups)

    def chunk(j, carry):
        back = 2 * half - CHUNK - j * CHUNK
        edge = jnp.where(j == 0, half, 2 * half - CHUNK * j)
        for g in everyone:
            fa[g] = images[g][pl.ds(pl.multiple_of(j * block, block), block), :].astype(jnp.float32)
            back_rows = pl.multiple_of(back * rows, block)
            fb[g, pl.ds(0, block), :] = images[g][pl.ds(back_rows, block), :].astype(jnp.float32)
            edge_rows = pl.multiple_of(edge * rows, block)
            fb[g, pl.ds(block, 2 * rows), :] = images[g][pl.ds(edge_rows, 2 * rows), :].astype(jnp.float32)
        paired = jnp.where(j == 0, 0.0, 1.0)
        for t in range(CHUNK):
            slot = t % left_ref.shape[0]
            for g in range(groups):
                a = fa[g, pl.ds(t * rows, rows), :]
                b = fb[g, pl.ds((CHUNK - t) * rows, rows), :]
                a_turned = pltpu.roll(a, cycles, 1) * sign
                b_turned = pltpu.roll(b, cycles, 1) * (-sign)
                if t == 0:
                    b_turned = b_turned * paired + b * (1.0 - paired)
                    a_turned = a_turned * paired
                    b = b * paired
                top = 2 * rows * g
                left_ref[slot, pl.ds(top, rows), pl.ds(0, LANES)] = a
                left_ref[slot, pl.ds(top, rows), pl.ds(LANES, LANES)] = b
                left_ref[slot, pl.ds(top + rows, rows), pl.ds(0, LANES)] = a_turned
                left_ref[slot, pl.ds(top + rows, rows), pl.ds(LANES, LANES)] = b_turned
            m = j * CHUNK + t
            mirror = edge if t == 0 else 2 * half - m
            right = jnp.concatenate(
                [
                    jnp.concatenate([ref[m] for ref in stacked], axis=0),
                    jnp.concatenate([ref[mirror] for ref in stacked], axis=0),
                ],
                axis=1,
            )
            folded[pl.ds(m * pitch, all_rows), :] = lax.dot_general(
                left_ref[slot].astype(jnp.bfloat16),
                right,
                (((1,), (1,)), ((), ())),
                preferred_element_type=jnp.float32,
            )
        return carry

    lax.fori_loop(0, steps, chunk, 0)
    table = table_ref[...]
    each = rows // shifts
    width = 2 * LANES

    def column(g, n):
        even = folded[pl.ds(2 * rows * g + n, half, stride=pitch), :]
        odd = folded[pl.ds(2 * rows * g + rows + n, half, stride=pitch), :]
        return jnp.concatenate([even, odd], axis=0).astype(jnp.bfloat16)

    def one_shift(s, best):
        better = []
        for q in range(groups * each // 2):
            columns = [column(i // each, s * each + i % each) for i in (2 * q, 2 * q + 1)]
            turned = jnp.dot(table, jnp.concatenate(columns, axis=1), preferred_element_type=jnp.float32)
            both = turned[:half] + jnp.abs(turned[half : 2 * half])
            top = jnp.max(both.reshape(half // 8, 8, width), axis=0)
            top = jnp.maximum(top, turned[2 * half :])
            better.append(jnp.maximum(best[q], top))
        return tuple(better)

    start = tuple(jnp.full((8, width), -jnp.inf, jnp.float32) for _ in range(groups * each // 2))
    best = lax.fori_loop(0, shifts, one_shift, start)
    for q in range(groups * each // 2):
        top = jnp.max(best[q], axis=0, keepdims=True) * scale
        first = places_ref[2 * q // each] * each + 2 * q % each
        out_ref[pl.ds(first, 1), :] = top[:, :LANES]
        out_ref[pl.ds(first + 1, 1), :] = top[:, LANES:]


def best_of_groups(places, images, stacked, table, shifts, rows, scale):
    angles, _, cycle_parts = stacked[0].shape
    half = angles // 2
    each = rows // shifts
    groups = len(images)
    flops = groups * (2 * half * 2 * rows * 2 * cycle_parts * LANES + 2 * rows * LANES * angles * (angles + 8))
    return pl.pallas_call(
        functools.partial(score_kernel, scale, rows, shifts, groups),
        in_specs=[SCALARS] + [WHOLE] * (groups + 3),
        out_specs=WHOLE,
        out_shape=jax.ShapeDtypeStruct((groups * each, LANES), jnp.float32),
        scratch_shapes=[
            pltpu.VMEM((4, 2 * rows * groups, 2 * cycle_parts), jnp.float32),
            pltpu.VMEM((groups, CHUNK * rows, cycle_parts), jnp.float32),
            pltpu.VMEM((groups, (CHUNK + 2) * rows, cycle_parts), jnp.float32),
            pltpu.VMEM(((2 * rows * groups + 1) * half, LANES), jnp.float32),
        ],
        compiler_params=pltpu.CompilerParams(vmem_limit_bytes=36 * 1024 * 1024),
        cost_estimate=pl.CostEstimate(flops=6 * flops, bytes_accessed=20_000_000, transcendentals=0),
        name="score",
    )(places, *images, *stacked, table)


def listing_kernel(shift_ref, id_ref, count_ref, weight_ref, images_ref, out_ref, work):
    own, length = id_ref.shape
    owners, tiles, depth, cycle_parts = out_ref.shape
    angles = owners * depth
    rows = images_ref.shape[0] // angles
    block = CHUNK * rows

    def widen(j, carry):
        part = pl.ds(pl.multiple_of(j * block, block), block)
        work[part, :] = images_ref[part, :].astype(jnp.float32)
        return carry

    lax.fori_loop(0, angles // CHUNK, widen, 0)
    lane = lax.broadcasted_iota(jnp.int32, (depth, cycle_parts), 1)
    digit = lax.broadcasted_iota(jnp.int32, (depth, cycle_parts), 0)
    notes = jnp.zeros((depth, cycle_parts), jnp.float32)
    for i in range(own):
        for j in range(length):
            place = i * length + j
            column = work[pl.ds(shift_ref[i, j] * own + i, angles, stride=rows), :]
            out_ref[:, place] = column.reshape(owners, depth, cycle_parts).astype(jnp.bfloat16)
            name = id_ref[i, j]
            kept = jnp.where(j < count_ref[i], weight_ref[i, j], 0.0)
            upper = (name >> 4).astype(jnp.float32)
            lower = (name & 15).astype(jnp.float32)
            value = jnp.where(digit == 0, upper, jnp.where(digit == 1, lower, jnp.where(digit == 2, kept, 0.0)))
            notes = jnp.where(lane == place, value, notes)
    out_ref[:, tiles - 1] = jnp.broadcast_to(notes.astype(jnp.bfloat16)[None], (owners, depth, cycle_parts))


def listings_by_owner(shift_ids, class_ids, counts, weights, images, owners):
    own, length = class_ids.shape
    cycle_parts = images.shape[1]
    rows = images.shape[0]
    angles = rows // (9 * own)
    shape = (owners, own * length + 1, angles // owners, cycle_parts)
    return pl.pallas_call(
        listing_kernel,
        in_specs=[SCALARS] * 4 + [WHOLE],
        out_specs=WHOLE,
        out_shape=jax.ShapeDtypeStruct(shape, jnp.bfloat16),
        scratch_shapes=[pltpu.VMEM((rows, cycle_parts), jnp.float32)],
        compiler_params=pltpu.CompilerParams(vmem_limit_bytes=14 * 1024 * 1024),
        cost_estimate=pl.CostEstimate(flops=0, bytes_accessed=8_000_000, transcendentals=0),
        name="listings",
    )(shift_ids, class_ids, counts, weights, images)


def sums_kernel(class_count, sets, arrived_ref, out_ref, work):
    sources, tiles, depth, cycle_parts = arrived_ref.shape
    listings = tiles - 1
    each = tiles * depth
    places = work.shape[0] // depth
    used = sources * each
    padded = -(-class_count // 8) * 8

    def widen(j, carry):
        first = pl.multiple_of(j * each, each)
        work[pl.ds(first, each), :] = arrived_ref[j].reshape(each, cycle_parts).astype(jnp.float32)
        return carry

    lax.fori_loop(0, sources, widen, 0)
    work[pl.ds(used, work.shape[0] - used), :] = jnp.zeros((work.shape[0] - used, cycle_parts), jnp.float32)
    lane = lax.broadcasted_iota(jnp.int32, (1, LANES), 1)
    names = [jnp.zeros((1, LANES), jnp.float32) for _ in range(places // LANES)]
    kept = [jnp.zeros((1, LANES), jnp.float32) for _ in range(places // LANES)]
    for source in range(sources):
        first = source * each + listings * depth
        name = work[pl.ds(first, 1), :] * 16.0 + work[pl.ds(first + 1, 1), :]
        weight = work[pl.ds(first + 2, 1), :]
        column, offset = divmod(source * tiles, LANES)
        if offset:
            name, weight = pltpu.roll(name, offset, 1), pltpu.roll(weight, offset, 1)
        here = lane >= offset
        names[column] = names[column] + jnp.where(here, name, 0.0)
        kept[column] = kept[column] + jnp.where(here, weight, 0.0)
        if offset + listings > LANES:
            names[column + 1] = names[column + 1] + jnp.where(here, 0.0, name)
            kept[column + 1] = kept[column + 1] + jnp.where(here, 0.0, weight)
    names = jnp.concatenate(names, axis=1)
    kept = jnp.concatenate(kept, axis=1)

    def mixing_of(block, rows):
        row = lax.broadcasted_iota(jnp.int32, (rows, places), 0)
        wanted = (row + block * class_count).astype(jnp.float32)
        return jnp.where((wanted == names) & (row < class_count), kept, 0.0).astype(jnp.bfloat16)

    mixing = jnp.concatenate([mixing_of(block, padded) for block in range(sets)], axis=0)
    ones = jnp.ones((8, places), jnp.bfloat16)
    for block in range(sets):
        total = lax.dot_general(
            ones, mixing_of(block, LANES), (((1,), (1,)), ((), ())), preferred_element_type=jnp.float32
        )
        out_ref[pl.ds((block * (class_count + 1) + class_count) * depth, depth), :] = total
    for m in range(0, depth, 2):
        pair = [work[pl.ds(m + k, places, stride=depth), :].astype(jnp.bfloat16) for k in range(2)]
        result = jnp.dot(mixing, jnp.concatenate(pair, axis=1), preferred_element_type=jnp.float32)
        for k in range(2):
            for block in range(sets):
                for first in range(0, class_count, 8):
                    n = min(8, class_count - first)
                    start = (block * (class_count + 1) + first) * depth + m + k
                    row = block * padded + first
                    out_ref[pl.ds(start, n, stride=depth), :] = result[
                        row : row + n, k * cycle_parts : (k + 1) * cycle_parts
                    ]


def class_shares(arrived, class_count, sets):
    sources, tiles, depth, cycle_parts = arrived.shape
    places = -(-sources * tiles // LANES) * LANES
    rows = sets * (class_count + 1) * depth
    return pl.pallas_call(
        functools.partial(sums_kernel, class_count, sets),
        in_specs=[WHOLE],
        out_specs=WHOLE,
        out_shape=jax.ShapeDtypeStruct((rows, cycle_parts), jnp.float32),
        scratch_shapes=[pltpu.VMEM((places * depth, cycle_parts), jnp.float32)],
        compiler_params=pltpu.CompilerParams(vmem_limit_bytes=14 * 1024 * 1024),
        cost_estimate=pl.CostEstimate(flops=4_000_000_000, bytes_accessed=8_000_000, transcendentals=0),
        name="shares",
    )(arrived)


def on_device(particles, references, class_ids, counts, shift_ids, weights):
    cls_index = lax.axis_index("cls")
    core = cls_index % 2
    row = cls_index // 2
    angles, own, shifts, cycle_parts = particles.shape
    class_count = references.shape[1]
    rows = shifts * own
    doms = 32
    chips = 4
    ring = 4
    scale = 1.0 / math.sqrt(1.0 * cycle_parts * angles)

    def move(value, target):
        pairs = [(2 * y + c, 2 * t + e) for y in range(chips) for c in range(2) for t, e in [target(y, c)]]
        return lax.ppermute(value, "cls", pairs)

    def across(value):
        return move(value, lambda y, c: (y, 1 - c))

    def facing(value):
        return move(value, lambda y, c: (chips - 1 - y, c))

    def around(value, step):
        length = doms // ring
        pairs = [(x * length + z, (x + step) % ring * length + z) for x in range(ring) for z in range(length)]
        return lax.ppermute(value, "dom", pairs)

    native = jnp.transpose(particles, (0, 2, 1, 3))
    flat = native.reshape(angles * rows, cycle_parts)
    class_major = jnp.transpose(references, (1, 0, 2))

    partner = move(flat, lambda y, c: (y ^ 1, c))
    mate = across(flat)
    partner_mate = across(partner)

    place = lax.axis_index("dom") // (doms // ring)
    window = class_count // ring
    straight = class_count - ring * window

    def window_of(x):
        return lax.dynamic_slice_in_dim(class_major, straight + window * x, window, 0)

    piece = facing(window_of(place))
    far = facing(jnp.concatenate([class_major[:straight], window_of((place + 2) % ring)]))
    from_left = around(piece, 1)
    from_right = around(piece, -1)

    own_set = by_harmonic([class_major], [(class_count,)], [0], LANES // 2)
    starts = [straight + window * ((place + step) % ring) for step in (2, 0, 3, 1)]
    facing_set = by_harmonic(
        [far, piece, from_left, from_right],
        [(straight, window)] + [(window,)] * 3,
        jnp.stack([jnp.zeros_like(place)] + starts),
        LANES // 2,
    )
    stacked = [own_set, facing_set]
    table = folded_table(angles)
    score = functools.partial(best_of_groups, stacked=stacked, table=table, shifts=shifts, rows=rows, scale=scale)

    depth = angles // doms
    payload = listings_by_owner(shift_ids, class_ids, counts, weights.astype(jnp.float32), flat, doms)
    tiles = payload.shape[1]
    arrived = lax.all_to_all(payload.reshape(doms, tiles * depth, cycle_parts), "dom", 0, 0, tiled=True)
    sums = class_shares(arrived.reshape(doms, tiles, depth, cycle_parts), class_count, 2 * chips)
    sums = sums.reshape(2 * chips, class_count + 1, depth, cycle_parts)
    shares = lax.all_to_all(sums, "cls", 0, 0, tiled=True)
    total = jnp.sum(shares, axis=0)
    weight_sums = total[class_count, 0, :class_count]
    class_means = total[:class_count] / jnp.maximum(weight_sums, 1.0)[:, None, None]
    class_means = jnp.transpose(class_means, (1, 0, 2))

    images = [flat, mate, partner, partner_mate]
    places = jnp.stack([(row % 2 ^ chip) * 2 + (core ^ other) for chip in range(2) for other in range(2)])
    best = score(places.astype(jnp.int32), images)
    sent = facing(best)
    mine, others = best[:, :class_count], sent[:, LANES // 2 : LANES // 2 + class_count]
    low = jnp.where(row < chips // 2, mine, others)
    high = jnp.where(row < chips // 2, others, mine)
    best_scores = jnp.concatenate([low, high], axis=0)
    return (best_scores, class_means)


def solution(mesh):
    return jax.shard_map(
        on_device,
        mesh=mesh,
        in_specs=(
            P(None, ("dom", "cls"), None, None),
            P(None, "cls", None),
            P(("dom", "cls"), None),
            P(("dom", "cls")),
            P(("dom", "cls"), None),
            P(("dom", "cls"), None),
        ),
        out_specs=(P("dom", "cls"), P("dom", "cls", None)),
        check_vma=False,
    )
```

```python
import functools
import math

import jax
import jax.numpy as jnp
from jax import lax
from jax.experimental import pallas as pl
from jax.experimental.pallas import tpu as pltpu
from jax.sharding import PartitionSpec as P


CHUNK = 16
LANES = 128
WHOLE = pl.BlockSpec(memory_space=pltpu.VMEM)
SCALARS = pl.BlockSpec(memory_space=pltpu.SMEM)


def folded_table(angles):
    half = angles // 2
    index = jnp.arange(half, dtype=jnp.int32)
    product = index[:, None] * index[None, :] % angles
    phase = product.astype(jnp.float32) * (2.0 * math.pi / angles)
    edge = (index[:, None] == 0) | (index[None, :] == 0)
    cosine = jnp.cos(phase)
    sine = jnp.where(edge, 0.0, -jnp.sin(phase))
    alternate = jnp.where(index % 2 == 0, 1.0, -1.0)
    nyquist = jnp.where(index[None, :] == 0, alternate[:, None], 0.0)
    last = jnp.concatenate([alternate, jnp.where(index == 0, 1.0, 0.0)])
    rows = [
        jnp.concatenate([cosine, nyquist], axis=1),
        jnp.concatenate([jnp.zeros_like(sine), sine], axis=1),
        jnp.broadcast_to(last[None, :], (8, angles)),
    ]
    return jnp.concatenate(rows, axis=0).astype(jnp.bfloat16)


def gather_kernel(sizes, starts_ref, *refs):
    pieces, out_ref, work = refs[: len(sizes)], refs[len(sizes)], refs[len(sizes) + 1]
    total = out_ref.shape[1]
    used = sum(map(sum, sizes))
    work[pl.ds(used * CHUNK, (total - used) * CHUNK), :] = jnp.zeros(((total - used) * CHUNK, LANES), jnp.float32)

    def chunk(j, carry):
        base = pl.multiple_of(j * CHUNK, CHUNK)
        k = 0
        for parts, ref in zip(sizes, pieces):
            above = 0
            for size in parts:
                block = ref[above : above + size, pl.ds(base, CHUNK), :].reshape(size * CHUNK, LANES)
                first = pl.multiple_of(starts_ref[k] * CHUNK, CHUNK)
                work[pl.ds(first, size * CHUNK), :] = block.astype(jnp.float32)
                above += size
                k += 1
        for t in range(CHUNK):
            out_ref[base + t] = work[pl.ds(t, total, stride=CHUNK), :].astype(jnp.bfloat16)
        return carry

    lax.fori_loop(0, out_ref.shape[0] // CHUNK, chunk, 0)


def by_harmonic(pieces, sizes, starts, total):
    angles, cycle_parts = pieces[0].shape[1:]
    moved = 2 * angles * cycle_parts * (sum(map(sum, sizes)) + total)
    return pl.pallas_call(
        functools.partial(gather_kernel, sizes),
        in_specs=[SCALARS] + [WHOLE] * len(pieces),
        out_specs=WHOLE,
        out_shape=jax.ShapeDtypeStruct((angles, total, cycle_parts), jnp.bfloat16),
        scratch_shapes=[pltpu.VMEM((total * CHUNK, cycle_parts), jnp.float32)],
        compiler_params=pltpu.CompilerParams(vmem_limit_bytes=14 * 1024 * 1024),
        cost_estimate=pl.CostEstimate(flops=0, bytes_accessed=2 * moved, transcendentals=0),
        name="by_harmonic",
    )(jnp.asarray(starts, jnp.int32), *pieces)


def score_kernel(scale, rows, shifts, counts, places_ref, *refs):
    groups = pieces = counts
    stacked = refs[pieces : pieces + 2]
    table_ref, out_ref, left_ref, fa, fb, folded = refs[pieces + 2 :]
    images = refs[:groups]
    half = table_ref.shape[1] // 2
    all_rows = 2 * rows * groups
    pitch = all_rows + 1
    cycles = LANES // 2
    lane = lax.broadcasted_iota(jnp.int32, (1, LANES), 1)
    sign = jnp.where(lane < cycles, 1.0, -1.0)
    block = CHUNK * rows
    steps = half // CHUNK

    everyone = range(groups)

    def chunk(j, carry):
        back = 2 * half - CHUNK - j * CHUNK
        edge = jnp.where(j == 0, half, 2 * half - CHUNK * j)
        for g in everyone:
            fa[g] = images[g][pl.ds(pl.multiple_of(j * block, block), block), :].astype(jnp.float32)
            back_rows = pl.multiple_of(back * rows, block)
            fb[g, pl.ds(0, block), :] = images[g][pl.ds(back_rows, block), :].astype(jnp.float32)
            edge_rows = pl.multiple_of(edge * rows, block)
            fb[g, pl.ds(block, 2 * rows), :] = images[g][pl.ds(edge_rows, 2 * rows), :].astype(jnp.float32)
        paired = jnp.where(j == 0, 0.0, 1.0)
        for t in range(CHUNK):
            slot = t % left_ref.shape[0]
            for g in range(groups):
                block_rows = pl.ds(rows * g, rows)
                left_ref[slot, block_rows, pl.ds(0, LANES)] = fa[g, pl.ds(t * rows, rows), :]
                left_ref[slot, block_rows, pl.ds(LANES, LANES)] = fb[g, pl.ds((CHUNK - t) * rows, rows), :]
            a = left_ref[slot, :, pl.ds(0, LANES)]
            b = left_ref[slot, :, pl.ds(LANES, LANES)]
            a_turned = pltpu.roll(a, cycles, 1) * sign
            b_turned = pltpu.roll(b, cycles, 1) * (-sign)
            if t == 0:
                b_turned = b_turned * paired + b * (1.0 - paired)
                a_turned = a_turned * paired
                b = b * paired
            straight = jnp.concatenate([a, b], axis=1).astype(jnp.bfloat16)
            turned = jnp.concatenate([a_turned, b_turned], axis=1).astype(jnp.bfloat16)
            left = jnp.concatenate([straight, turned], axis=0)
            m = j * CHUNK + t
            mirror = edge if t == 0 else 2 * half - m
            right = jnp.concatenate(
                [
                    jnp.concatenate([ref[m] for ref in stacked], axis=0),
                    jnp.concatenate([ref[mirror] for ref in stacked], axis=0),
                ],
                axis=1,
            )
            folded[pl.ds(m * pitch, all_rows), :] = lax.dot_general(
                left,
                right,
                (((1,), (1,)), ((), ())),
                preferred_element_type=jnp.float32,
            )
        return carry

    lax.fori_loop(0, steps, chunk, 0)
    table = table_ref[...]
    each = rows // shifts
    width = 2 * LANES

    def column(g, n):
        even = folded[pl.ds(rows * g + n, half, stride=pitch), :]
        odd = folded[pl.ds(rows * (groups + g) + n, half, stride=pitch), :]
        return jnp.concatenate([even, odd], axis=0).astype(jnp.bfloat16)

    def one_shift(s, best):
        better = []
        for q in range(groups * each // 2):
            columns = [column(i // each, s * each + i % each) for i in (2 * q, 2 * q + 1)]
            turned = jnp.dot(table, jnp.concatenate(columns, axis=1), preferred_element_type=jnp.float32)
            both = turned[:half] + jnp.abs(turned[half : 2 * half])
            top = jnp.max(both.reshape(half // 8, 8, width), axis=0)
            top = jnp.maximum(top, turned[2 * half :])
            better.append(jnp.maximum(best[q], top))
        return tuple(better)

    start = tuple(jnp.full((8, width), -jnp.inf, jnp.float32) for _ in range(groups * each // 2))
    best = lax.fori_loop(0, shifts, one_shift, start)
    for q in range(groups * each // 2):
        top = jnp.max(best[q], axis=0, keepdims=True) * scale
        first = places_ref[2 * q // each] * each + 2 * q % each
        out_ref[pl.ds(first, 1), :] = top[:, :LANES]
        out_ref[pl.ds(first + 1, 1), :] = top[:, LANES:]


def best_of_groups(places, images, stacked, table, shifts, rows, scale):
    angles, _, cycle_parts = stacked[0].shape
    half = angles // 2
    each = rows // shifts
    groups = len(images)
    flops = groups * (2 * half * 2 * rows * 2 * cycle_parts * LANES + 2 * rows * LANES * angles * (angles + 8))
    return pl.pallas_call(
        functools.partial(score_kernel, scale, rows, shifts, groups),
        in_specs=[SCALARS] + [WHOLE] * (groups + 3),
        out_specs=WHOLE,
        out_shape=jax.ShapeDtypeStruct((groups * each, LANES), jnp.float32),
        scratch_shapes=[
            pltpu.VMEM((4, rows * groups, 2 * cycle_parts), jnp.float32),
            pltpu.VMEM((groups, CHUNK * rows, cycle_parts), jnp.float32),
            pltpu.VMEM((groups, (CHUNK + 2) * rows, cycle_parts), jnp.float32),
            pltpu.VMEM(((2 * rows * groups + 1) * half, LANES), jnp.float32),
        ],
        compiler_params=pltpu.CompilerParams(vmem_limit_bytes=36 * 1024 * 1024),
        cost_estimate=pl.CostEstimate(flops=6 * flops, bytes_accessed=20_000_000, transcendentals=0),
        name="score",
    )(places, *images, *stacked, table)


def listing_kernel(shift_ref, id_ref, count_ref, weight_ref, images_ref, out_ref, work):
    own, length = id_ref.shape
    owners, tiles, depth, cycle_parts = out_ref.shape
    angles = owners * depth
    rows = images_ref.shape[0] // angles
    block = CHUNK * rows

    def widen(j, carry):
        part = pl.ds(pl.multiple_of(j * block, block), block)
        work[part, :] = images_ref[part, :].astype(jnp.float32)
        return carry

    lax.fori_loop(0, angles // CHUNK, widen, 0)
    lane = lax.broadcasted_iota(jnp.int32, (depth, cycle_parts), 1)
    digit = lax.broadcasted_iota(jnp.int32, (depth, cycle_parts), 0)
    notes = jnp.zeros((depth, cycle_parts), jnp.float32)
    for i in range(own):
        for j in range(length):
            place = i * length + j
            column = work[pl.ds(shift_ref[i, j] * own + i, angles, stride=rows), :]
            out_ref[:, place] = column.reshape(owners, depth, cycle_parts).astype(jnp.bfloat16)
            name = id_ref[i, j]
            kept = jnp.where(j < count_ref[i], weight_ref[i, j], 0.0)
            upper = (name >> 4).astype(jnp.float32)
            lower = (name & 15).astype(jnp.float32)
            value = jnp.where(digit == 0, upper, jnp.where(digit == 1, lower, jnp.where(digit == 2, kept, 0.0)))
            notes = jnp.where(lane == place, value, notes)
    out_ref[:, tiles - 1] = jnp.broadcast_to(notes.astype(jnp.bfloat16)[None], (owners, depth, cycle_parts))


def listings_by_owner(shift_ids, class_ids, counts, weights, images, owners):
    own, length = class_ids.shape
    cycle_parts = images.shape[1]
    rows = images.shape[0]
    angles = rows // (9 * own)
    shape = (owners, own * length + 1, angles // owners, cycle_parts)
    return pl.pallas_call(
        listing_kernel,
        in_specs=[SCALARS] * 4 + [WHOLE],
        out_specs=WHOLE,
        out_shape=jax.ShapeDtypeStruct(shape, jnp.bfloat16),
        scratch_shapes=[pltpu.VMEM((rows, cycle_parts), jnp.float32)],
        compiler_params=pltpu.CompilerParams(vmem_limit_bytes=14 * 1024 * 1024),
        cost_estimate=pl.CostEstimate(flops=0, bytes_accessed=8_000_000, transcendentals=0),
        name="listings",
    )(shift_ids, class_ids, counts, weights, images)


def sums_kernel(class_count, sets, arrived_ref, out_ref, work):
    sources, tiles, depth, cycle_parts = arrived_ref.shape
    listings = tiles - 1
    each = tiles * depth
    places = work.shape[0] // depth
    used = sources * each
    padded = -(-class_count // 8) * 8

    def widen(j, carry):
        first = pl.multiple_of(j * each, each)
        work[pl.ds(first, each), :] = arrived_ref[j].reshape(each, cycle_parts).astype(jnp.float32)
        return carry

    lax.fori_loop(0, sources, widen, 0)
    work[pl.ds(used, work.shape[0] - used), :] = jnp.zeros((work.shape[0] - used, cycle_parts), jnp.float32)
    lane = lax.broadcasted_iota(jnp.int32, (1, LANES), 1)
    names = [jnp.zeros((1, LANES), jnp.float32) for _ in range(places // LANES)]
    kept = [jnp.zeros((1, LANES), jnp.float32) for _ in range(places // LANES)]
    for source in range(sources):
        first = source * each + listings * depth
        name = work[pl.ds(first, 1), :] * 16.0 + work[pl.ds(first + 1, 1), :]
        weight = work[pl.ds(first + 2, 1), :]
        column, offset = divmod(source * tiles, LANES)
        if offset:
            name, weight = pltpu.roll(name, offset, 1), pltpu.roll(weight, offset, 1)
        here = lane >= offset
        names[column] = names[column] + jnp.where(here, name, 0.0)
        kept[column] = kept[column] + jnp.where(here, weight, 0.0)
        if offset + listings > LANES:
            names[column + 1] = names[column + 1] + jnp.where(here, 0.0, name)
            kept[column + 1] = kept[column + 1] + jnp.where(here, 0.0, weight)
    names = jnp.concatenate(names, axis=1)
    kept = jnp.concatenate(kept, axis=1)

    def mixing_of(block, rows):
        row = lax.broadcasted_iota(jnp.int32, (rows, places), 0)
        wanted = (row + block * class_count).astype(jnp.float32)
        return jnp.where((wanted == names) & (row < class_count), kept, 0.0).astype(jnp.bfloat16)

    mixing = jnp.concatenate([mixing_of(block, padded) for block in range(sets)], axis=0)
    ones = jnp.ones((8, places), jnp.bfloat16)
    for block in range(sets):
        total = lax.dot_general(
            ones, mixing_of(block, LANES), (((1,), (1,)), ((), ())), preferred_element_type=jnp.float32
        )
        out_ref[pl.ds((block * (class_count + 1) + class_count) * depth, depth), :] = total
    for m in range(0, depth, 2):
        pair = [work[pl.ds(m + k, places, stride=depth), :].astype(jnp.bfloat16) for k in range(2)]
        result = jnp.dot(mixing, jnp.concatenate(pair, axis=1), preferred_element_type=jnp.float32)
        for k in range(2):
            for block in range(sets):
                for first in range(0, class_count, 8):
                    n = min(8, class_count - first)
                    start = (block * (class_count + 1) + first) * depth + m + k
                    row = block * padded + first
                    out_ref[pl.ds(start, n, stride=depth), :] = result[
                        row : row + n, k * cycle_parts : (k + 1) * cycle_parts
                    ]


def class_shares(arrived, class_count, sets):
    sources, tiles, depth, cycle_parts = arrived.shape
    places = -(-sources * tiles // LANES) * LANES
    rows = sets * (class_count + 1) * depth
    return pl.pallas_call(
        functools.partial(sums_kernel, class_count, sets),
        in_specs=[WHOLE],
        out_specs=WHOLE,
        out_shape=jax.ShapeDtypeStruct((rows, cycle_parts), jnp.float32),
        scratch_shapes=[pltpu.VMEM((places * depth, cycle_parts), jnp.float32)],
        compiler_params=pltpu.CompilerParams(vmem_limit_bytes=14 * 1024 * 1024),
        cost_estimate=pl.CostEstimate(flops=4_000_000_000, bytes_accessed=8_000_000, transcendentals=0),
        name="shares",
    )(arrived)


def means_kernel(shares_ref, out_ref):
    sources, extended, depth, cycle_parts = shares_ref.shape
    class_count = extended - 1
    lane = lax.broadcasted_iota(jnp.int32, (depth, cycle_parts), 1)

    def summed(k):
        total = shares_ref[0, k]
        for source in range(1, sources):
            total = total + shares_ref[source, k]
        return total

    weights = jnp.maximum(summed(class_count), 1.0)
    for k in range(class_count):
        weight = jnp.sum(jnp.where(lane == k, weights, 0.0), axis=1, keepdims=True)
        out_ref[k] = summed(k) / weight


def means_of(shares):
    _, extended, depth, cycle_parts = shares.shape
    return pl.pallas_call(
        means_kernel,
        in_specs=[WHOLE],
        out_specs=WHOLE,
        out_shape=jax.ShapeDtypeStruct((extended - 1, depth, cycle_parts), jnp.float32),
        compiler_params=pltpu.CompilerParams(vmem_limit_bytes=6 * 1024 * 1024),
        cost_estimate=pl.CostEstimate(flops=500_000, bytes_accessed=2_000_000, transcendentals=0),
        name="means",
    )(shares)


def on_device(particles, references, class_ids, counts, shift_ids, weights):
    cls_index = lax.axis_index("cls")
    core = cls_index % 2
    row = cls_index // 2
    angles, own, shifts, cycle_parts = particles.shape
    class_count = references.shape[1]
    rows = shifts * own
    doms = 32
    chips = 4
    ring = 4
    scale = 1.0 / math.sqrt(1.0 * cycle_parts * angles)

    def move(value, target):
        pairs = [(2 * y + c, 2 * t + e) for y in range(chips) for c in range(2) for t, e in [target(y, c)]]
        return lax.ppermute(value, "cls", pairs)

    def across(value):
        return move(value, lambda y, c: (y, 1 - c))

    def facing(value):
        return move(value, lambda y, c: (chips - 1 - y, c))

    def around(value, step):
        length = doms // ring
        pairs = [(x * length + z, (x + step) % ring * length + z) for x in range(ring) for z in range(length)]
        return lax.ppermute(value, "dom", pairs)

    native = jnp.transpose(particles, (0, 2, 1, 3))
    flat = native.reshape(angles * rows, cycle_parts)
    class_major = jnp.transpose(references, (1, 0, 2))

    partner = move(flat, lambda y, c: (y ^ 1, c))
    mate = across(flat)
    partner_mate = across(partner)

    place = lax.axis_index("dom") // (doms // ring)
    window = class_count // ring
    straight = class_count - ring * window

    def window_of(x):
        return lax.dynamic_slice_in_dim(class_major, straight + window * x, window, 0)

    piece = facing(window_of(place))
    far = facing(jnp.concatenate([class_major[:straight], window_of((place + 2) % ring)]))
    from_left = around(piece, 1)
    from_right = around(piece, -1)

    own_set = by_harmonic([class_major], [(class_count,)], [0], LANES // 2)
    starts = [straight + window * ((place + step) % ring) for step in (2, 0, 3, 1)]
    facing_set = by_harmonic(
        [far, piece, from_left, from_right],
        [(straight, window)] + [(window,)] * 3,
        jnp.stack([jnp.zeros_like(place)] + starts),
        LANES // 2,
    )
    stacked = [own_set, facing_set]
    table = folded_table(angles)
    score = functools.partial(best_of_groups, stacked=stacked, table=table, shifts=shifts, rows=rows, scale=scale)

    depth = angles // doms
    payload = listings_by_owner(shift_ids, class_ids, counts, weights.astype(jnp.float32), flat, doms)
    tiles = payload.shape[1]
    arrived = lax.all_to_all(payload.reshape(doms, tiles * depth, cycle_parts), "dom", 0, 0, tiled=True)
    sums = class_shares(arrived.reshape(doms, tiles, depth, cycle_parts), class_count, 2 * chips)
    sums = sums.reshape(2 * chips, class_count + 1, depth, cycle_parts)
    shares = lax.all_to_all(sums, "cls", 0, 0, tiled=True)
    class_means = means_of(shares)
    class_means = jnp.transpose(class_means, (1, 0, 2))

    images = [flat, mate, partner, partner_mate]
    places = jnp.stack([(row % 2 ^ chip) * 2 + (core ^ other) for chip in range(2) for other in range(2)])
    best = score(places.astype(jnp.int32), images)
    sent = facing(best)
    mine, others = best[:, :class_count], sent[:, LANES // 2 : LANES // 2 + class_count]
    low = jnp.where(row < chips // 2, mine, others)
    high = jnp.where(row < chips // 2, others, mine)
    best_scores = jnp.concatenate([low, high], axis=0)
    return (best_scores, class_means)


def solution(mesh):
    return jax.shard_map(
        on_device,
        mesh=mesh,
        in_specs=(
            P(None, ("dom", "cls"), None, None),
            P(None, "cls", None),
            P(("dom", "cls"), None),
            P(("dom", "cls")),
            P(("dom", "cls"), None),
            P(("dom", "cls"), None),
        ),
        out_specs=(P("dom", "cls"), P("dom", "cls", None)),
        check_vma=False,
    )
```

```python
import functools
import math

import jax
import jax.numpy as jnp
from jax import lax
from jax.experimental import pallas as pl
from jax.experimental.pallas import tpu as pltpu
from jax.sharding import PartitionSpec as P


CHUNK = 16
SCORE_CHUNK = 32
PITCH = CHUNK + 8
LANES = 128
WHOLE = pl.BlockSpec(memory_space=pltpu.VMEM)
SCALARS = pl.BlockSpec(memory_space=pltpu.SMEM)


def folded_table(angles):
    half = angles // 2
    index = jnp.arange(half, dtype=jnp.int32)
    product = index[:, None] * index[None, :] % angles
    phase = product.astype(jnp.float32) * (2.0 * math.pi / angles)
    edge = (index[:, None] == 0) | (index[None, :] == 0)
    cosine = jnp.cos(phase)
    sine = jnp.where(edge, 0.0, -jnp.sin(phase))
    alternate = jnp.where(index % 2 == 0, 1.0, -1.0)
    nyquist = jnp.where(index[None, :] == 0, alternate[:, None], 0.0)
    last = jnp.concatenate([alternate, jnp.where(index == 0, 1.0, 0.0)])
    rows = [
        jnp.concatenate([cosine, nyquist], axis=1),
        jnp.concatenate([jnp.zeros_like(sine), sine], axis=1),
        jnp.broadcast_to(last[None, :], (8, angles)),
    ]
    return jnp.concatenate(rows, axis=0).astype(jnp.bfloat16)


def gather_kernel(sizes, starts_ref, *refs):
    pieces, out_ref, work = refs[: len(sizes)], refs[len(sizes)], refs[len(sizes) + 1]
    total = out_ref.shape[1]
    used = sum(map(sum, sizes))
    work[pl.ds(used * PITCH, (total - used) * PITCH), :] = jnp.zeros(((total - used) * PITCH, LANES), jnp.float32)

    def chunk(j, carry):
        base = pl.multiple_of(j * CHUNK, CHUNK)
        k = 0
        for parts, ref in zip(sizes, pieces):
            above = 0
            for size in parts:
                for row in range(size):
                    first = pl.multiple_of((starts_ref[k] + row) * PITCH, 8)
                    work[pl.ds(first, CHUNK), :] = ref[above + row, pl.ds(base, CHUNK), :].astype(jnp.float32)
                above += size
                k += 1
        for t in range(CHUNK):
            out_ref[base + t] = work[pl.ds(t, total, stride=PITCH), :].astype(jnp.bfloat16)
        return carry

    lax.fori_loop(0, out_ref.shape[0] // CHUNK, chunk, 0)


def by_harmonic(pieces, sizes, starts, total):
    angles, cycle_parts = pieces[0].shape[1:]
    moved = 2 * angles * cycle_parts * (sum(map(sum, sizes)) + total)
    return pl.pallas_call(
        functools.partial(gather_kernel, sizes),
        in_specs=[SCALARS] + [WHOLE] * len(pieces),
        out_specs=WHOLE,
        out_shape=jax.ShapeDtypeStruct((angles, total, cycle_parts), jnp.bfloat16),
        scratch_shapes=[pltpu.VMEM((total * PITCH, cycle_parts), jnp.float32)],
        compiler_params=pltpu.CompilerParams(vmem_limit_bytes=14 * 1024 * 1024),
        cost_estimate=pl.CostEstimate(flops=0, bytes_accessed=2 * moved, transcendentals=0),
        name="by_harmonic",
    )(jnp.asarray(starts, jnp.int32), *pieces)


def score_kernel(scale, rows, shifts, counts, places_ref, *refs):
    groups = pieces = counts
    stacked = refs[pieces : pieces + 2]
    table_ref, out_ref, left_ref, fa, fb, folded = refs[pieces + 2 :]
    images = refs[:groups]
    half = table_ref.shape[1] // 2
    all_rows = 2 * rows * groups
    pitch = all_rows + 1
    cycles = LANES // 2
    lane = lax.broadcasted_iota(jnp.int32, (1, LANES), 1)
    sign = jnp.where(lane < cycles, 1.0, -1.0)
    block = SCORE_CHUNK * rows
    steps = half // SCORE_CHUNK

    everyone = range(groups)

    def chunk(j, carry):
        back = 2 * half - SCORE_CHUNK - j * SCORE_CHUNK
        edge = jnp.where(j == 0, half, 2 * half - SCORE_CHUNK * j)
        for g in everyone:
            fa[g] = images[g][pl.ds(pl.multiple_of(j * block, block), block), :].astype(jnp.float32)
            back_rows = pl.multiple_of(back * rows, block)
            fb[g, pl.ds(0, block), :] = images[g][pl.ds(back_rows, block), :].astype(jnp.float32)
            edge_rows = pl.multiple_of(edge * rows, block)
            fb[g, pl.ds(block, 2 * rows), :] = images[g][pl.ds(edge_rows, 2 * rows), :].astype(jnp.float32)
        paired = jnp.where(j == 0, 0.0, 1.0)
        for t in range(SCORE_CHUNK):
            slot = t % left_ref.shape[0]
            for g in range(groups):
                block_rows = pl.ds(rows * g, rows)
                left_ref[slot, block_rows, pl.ds(0, LANES)] = fa[g, pl.ds(t * rows, rows), :]
                left_ref[slot, block_rows, pl.ds(LANES, LANES)] = fb[g, pl.ds((SCORE_CHUNK - t) * rows, rows), :]
            a = left_ref[slot, :, pl.ds(0, LANES)]
            b = left_ref[slot, :, pl.ds(LANES, LANES)]
            a_turned = pltpu.roll(a, cycles, 1) * sign
            b_turned = pltpu.roll(b, cycles, 1) * (-sign)
            if t == 0:
                b_turned = b_turned * paired + b * (1.0 - paired)
                a_turned = a_turned * paired
                b = b * paired
            straight = jnp.concatenate([a, b], axis=1).astype(jnp.bfloat16)
            turned = jnp.concatenate([a_turned, b_turned], axis=1).astype(jnp.bfloat16)
            left = jnp.concatenate([straight, turned], axis=0)
            m = j * SCORE_CHUNK + t
            mirror = edge if t == 0 else 2 * half - m
            right = jnp.concatenate(
                [
                    jnp.concatenate([ref[m] for ref in stacked], axis=0),
                    jnp.concatenate([ref[mirror] for ref in stacked], axis=0),
                ],
                axis=1,
            )
            folded[pl.ds(m * pitch, all_rows), :] = lax.dot_general(
                left,
                right,
                (((1,), (1,)), ((), ())),
                preferred_element_type=jnp.float32,
            )
        return carry

    lax.fori_loop(0, steps, chunk, 0)
    table = table_ref[...]
    each = rows // shifts
    width = 2 * LANES

    def column(g, n):
        even = folded[pl.ds(rows * g + n, half, stride=pitch), :]
        odd = folded[pl.ds(rows * (groups + g) + n, half, stride=pitch), :]
        return jnp.concatenate([even, odd], axis=0).astype(jnp.bfloat16)

    def one_shift(s, best):
        better = []
        for q in range(groups * each // 2):
            columns = [column(i // each, s * each + i % each) for i in (2 * q, 2 * q + 1)]
            turned = jnp.dot(table, jnp.concatenate(columns, axis=1), preferred_element_type=jnp.float32)
            both = turned[:half] + jnp.abs(turned[half : 2 * half])
            top = jnp.max(both.reshape(half // 8, 8, width), axis=0)
            top = jnp.maximum(top, turned[2 * half :])
            better.append(jnp.maximum(best[q], top))
        return tuple(better)

    start = tuple(jnp.full((8, width), -jnp.inf, jnp.float32) for _ in range(groups * each // 2))
    best = lax.fori_loop(0, shifts, one_shift, start)
    for q in range(groups * each // 2):
        top = jnp.max(best[q], axis=0, keepdims=True) * scale
        first = places_ref[2 * q // each] * each + 2 * q % each
        out_ref[pl.ds(first, 1), :] = top[:, :LANES]
        out_ref[pl.ds(first + 1, 1), :] = top[:, LANES:]


def best_of_groups(places, images, stacked, table, shifts, rows, scale):
    angles, _, cycle_parts = stacked[0].shape
    half = angles // 2
    each = rows // shifts
    groups = len(images)
    flops = groups * (2 * half * 2 * rows * 2 * cycle_parts * LANES + 2 * rows * LANES * angles * (angles + 8))
    return pl.pallas_call(
        functools.partial(score_kernel, scale, rows, shifts, groups),
        in_specs=[SCALARS] + [WHOLE] * (groups + 3),
        out_specs=WHOLE,
        out_shape=jax.ShapeDtypeStruct((groups * each, LANES), jnp.float32),
        scratch_shapes=[
            pltpu.VMEM((4, rows * groups, 2 * cycle_parts), jnp.float32),
            pltpu.VMEM((groups, SCORE_CHUNK * rows, cycle_parts), jnp.float32),
            pltpu.VMEM((groups, (SCORE_CHUNK + 2) * rows, cycle_parts), jnp.float32),
            pltpu.VMEM(((2 * rows * groups + 1) * half, LANES), jnp.float32),
        ],
        compiler_params=pltpu.CompilerParams(vmem_limit_bytes=36 * 1024 * 1024),
        cost_estimate=pl.CostEstimate(flops=6 * flops, bytes_accessed=20_000_000, transcendentals=0),
        name="score",
    )(places, *images, *stacked, table)


def listing_kernel(shift_ref, id_ref, count_ref, weight_ref, images_ref, out_ref, work):
    own, length = id_ref.shape
    owners, tiles, depth, cycle_parts = out_ref.shape
    angles = owners * depth
    rows = images_ref.shape[0] // angles
    block = CHUNK * rows

    def widen(j, carry):
        part = pl.ds(pl.multiple_of(j * block, block), block)
        work[part, :] = images_ref[part, :].astype(jnp.float32)
        return carry

    lax.fori_loop(0, angles // CHUNK, widen, 0)
    lane = lax.broadcasted_iota(jnp.int32, (depth, cycle_parts), 1)
    digit = lax.broadcasted_iota(jnp.int32, (depth, cycle_parts), 0)
    notes = jnp.zeros((depth, cycle_parts), jnp.float32)
    for i in range(own):
        for j in range(length):
            place = i * length + j
            column = work[pl.ds(shift_ref[i, j] * own + i, angles, stride=rows), :]
            out_ref[:, place] = column.reshape(owners, depth, cycle_parts).astype(jnp.bfloat16)
            name = id_ref[i, j]
            kept = jnp.where(j < count_ref[i], weight_ref[i, j], 0.0)
            upper = (name >> 4).astype(jnp.float32)
            lower = (name & 15).astype(jnp.float32)
            value = jnp.where(digit == 0, upper, jnp.where(digit == 1, lower, jnp.where(digit == 2, kept, 0.0)))
            notes = jnp.where(lane == place, value, notes)
    out_ref[:, tiles - 1] = jnp.broadcast_to(notes.astype(jnp.bfloat16)[None], (owners, depth, cycle_parts))


def listings_by_owner(shift_ids, class_ids, counts, weights, images, owners):
    own, length = class_ids.shape
    cycle_parts = images.shape[1]
    rows = images.shape[0]
    angles = rows // (9 * own)
    shape = (owners, own * length + 1, angles // owners, cycle_parts)
    return pl.pallas_call(
        listing_kernel,
        in_specs=[SCALARS] * 4 + [WHOLE],
        out_specs=WHOLE,
        out_shape=jax.ShapeDtypeStruct(shape, jnp.bfloat16),
        scratch_shapes=[pltpu.VMEM((rows, cycle_parts), jnp.float32)],
        compiler_params=pltpu.CompilerParams(vmem_limit_bytes=14 * 1024 * 1024),
        cost_estimate=pl.CostEstimate(flops=0, bytes_accessed=8_000_000, transcendentals=0),
        name="listings",
    )(shift_ids, class_ids, counts, weights, images)


def sums_kernel(class_count, sets, arrived_ref, out_ref, work):
    sources, tiles, depth, cycle_parts = arrived_ref.shape
    listings = tiles - 1
    each = tiles * depth
    places = work.shape[0] // depth
    used = sources * each
    padded = -(-class_count // 8) * 8

    def widen(j, carry):
        first = pl.multiple_of(j * each, each)
        work[pl.ds(first, each), :] = arrived_ref[j].reshape(each, cycle_parts).astype(jnp.float32)
        return carry

    lax.fori_loop(0, sources, widen, 0)
    work[pl.ds(used, work.shape[0] - used), :] = jnp.zeros((work.shape[0] - used, cycle_parts), jnp.float32)
    lane = lax.broadcasted_iota(jnp.int32, (1, LANES), 1)
    names = [jnp.zeros((1, LANES), jnp.float32) for _ in range(places // LANES)]
    kept = [jnp.zeros((1, LANES), jnp.float32) for _ in range(places // LANES)]
    for source in range(sources):
        first = source * each + listings * depth
        name = work[pl.ds(first, 1), :] * 16.0 + work[pl.ds(first + 1, 1), :]
        weight = work[pl.ds(first + 2, 1), :]
        column, offset = divmod(source * tiles, LANES)
        if offset:
            name, weight = pltpu.roll(name, offset, 1), pltpu.roll(weight, offset, 1)
        here = lane >= offset
        names[column] = names[column] + jnp.where(here, name, 0.0)
        kept[column] = kept[column] + jnp.where(here, weight, 0.0)
        if offset + listings > LANES:
            names[column + 1] = names[column + 1] + jnp.where(here, 0.0, name)
            kept[column + 1] = kept[column + 1] + jnp.where(here, 0.0, weight)
    names = jnp.concatenate(names, axis=1)
    kept = jnp.concatenate(kept, axis=1)

    def mixing_of(block, rows):
        row = lax.broadcasted_iota(jnp.int32, (rows, places), 0)
        wanted = (row + block * class_count).astype(jnp.float32)
        return jnp.where((wanted == names) & (row < class_count), kept, 0.0).astype(jnp.bfloat16)

    mixing = jnp.concatenate([mixing_of(block, padded) for block in range(sets)], axis=0)
    ones = jnp.ones((8, places), jnp.bfloat16)
    for block in range(sets):
        total = lax.dot_general(
            ones, mixing_of(block, LANES), (((1,), (1,)), ((), ())), preferred_element_type=jnp.float32
        )
        out_ref[pl.ds((block * (class_count + 1) + class_count) * depth, depth), :] = total
    for m in range(0, depth, 2):
        pair = [work[pl.ds(m + k, places, stride=depth), :].astype(jnp.bfloat16) for k in range(2)]
        result = jnp.dot(mixing, jnp.concatenate(pair, axis=1), preferred_element_type=jnp.float32)
        for k in range(2):
            for block in range(sets):
                for first in range(0, class_count, 8):
                    n = min(8, class_count - first)
                    start = (block * (class_count + 1) + first) * depth + m + k
                    row = block * padded + first
                    out_ref[pl.ds(start, n, stride=depth), :] = result[
                        row : row + n, k * cycle_parts : (k + 1) * cycle_parts
                    ]


def class_shares(arrived, class_count, sets):
    sources, tiles, depth, cycle_parts = arrived.shape
    places = -(-sources * tiles // LANES) * LANES
    rows = sets * (class_count + 1) * depth
    return pl.pallas_call(
        functools.partial(sums_kernel, class_count, sets),
        in_specs=[WHOLE],
        out_specs=WHOLE,
        out_shape=jax.ShapeDtypeStruct((rows, cycle_parts), jnp.float32),
        scratch_shapes=[pltpu.VMEM((places * depth, cycle_parts), jnp.float32)],
        compiler_params=pltpu.CompilerParams(vmem_limit_bytes=14 * 1024 * 1024),
        cost_estimate=pl.CostEstimate(flops=4_000_000_000, bytes_accessed=8_000_000, transcendentals=0),
        name="shares",
    )(arrived)


def means_kernel(shares_ref, out_ref):
    sources, extended, depth, cycle_parts = shares_ref.shape
    class_count = extended - 1
    lane = lax.broadcasted_iota(jnp.int32, (depth, cycle_parts), 1)

    def summed(k):
        total = shares_ref[0, k]
        for source in range(1, sources):
            total = total + shares_ref[source, k]
        return total

    weights = jnp.maximum(summed(class_count), 1.0)
    for k in range(class_count):
        weight = jnp.sum(jnp.where(lane == k, weights, 0.0), axis=1, keepdims=True)
        out_ref[k] = summed(k) / weight


def means_of(shares):
    _, extended, depth, cycle_parts = shares.shape
    return pl.pallas_call(
        means_kernel,
        in_specs=[WHOLE],
        out_specs=WHOLE,
        out_shape=jax.ShapeDtypeStruct((extended - 1, depth, cycle_parts), jnp.float32),
        compiler_params=pltpu.CompilerParams(vmem_limit_bytes=6 * 1024 * 1024),
        cost_estimate=pl.CostEstimate(flops=500_000, bytes_accessed=2_000_000, transcendentals=0),
        name="means",
    )(shares)


def on_device(particles, references, class_ids, counts, shift_ids, weights):
    cls_index = lax.axis_index("cls")
    core = cls_index % 2
    row = cls_index // 2
    angles, own, shifts, cycle_parts = particles.shape
    class_count = references.shape[1]
    rows = shifts * own
    doms = 32
    chips = 4
    ring = 4
    scale = 1.0 / math.sqrt(1.0 * cycle_parts * angles)

    def move(value, target):
        pairs = [(2 * y + c, 2 * t + e) for y in range(chips) for c in range(2) for t, e in [target(y, c)]]
        return lax.ppermute(value, "cls", pairs)

    def across(value):
        return move(value, lambda y, c: (y, 1 - c))

    def facing(value):
        return move(value, lambda y, c: (chips - 1 - y, c))

    def around(value, step):
        length = doms // ring
        pairs = [(x * length + z, (x + step) % ring * length + z) for x in range(ring) for z in range(length)]
        return lax.ppermute(value, "dom", pairs)

    native = jnp.transpose(particles, (0, 2, 1, 3))
    flat = native.reshape(angles * rows, cycle_parts)
    class_major = jnp.transpose(references, (1, 0, 2))

    partner = move(flat, lambda y, c: (y ^ 1, c))
    mate = across(flat)
    partner_mate = across(partner)

    place = lax.axis_index("dom") // (doms // ring)
    window = class_count // ring
    straight = class_count - ring * window

    def window_of(x):
        return lax.dynamic_slice_in_dim(class_major, straight + window * x, window, 0)

    piece = facing(window_of(place))
    far = facing(jnp.concatenate([class_major[:straight], window_of((place + 2) % ring)]))
    from_left = around(piece, 1)
    from_right = around(piece, -1)

    own_set = by_harmonic([class_major], [(class_count,)], [0], LANES // 2)
    starts = [straight + window * ((place + step) % ring) for step in (2, 0, 3, 1)]
    facing_set = by_harmonic(
        [far, piece, from_left, from_right],
        [(straight, window)] + [(window,)] * 3,
        jnp.stack([jnp.zeros_like(place)] + starts),
        LANES // 2,
    )
    stacked = [own_set, facing_set]
    table = folded_table(angles)
    score = functools.partial(best_of_groups, stacked=stacked, table=table, shifts=shifts, rows=rows, scale=scale)

    depth = angles // doms
    payload = listings_by_owner(shift_ids, class_ids, counts, weights.astype(jnp.float32), flat, doms)
    tiles = payload.shape[1]
    arrived = lax.all_to_all(payload.reshape(doms, tiles * depth, cycle_parts), "dom", 0, 0, tiled=True)
    sums = class_shares(arrived.reshape(doms, tiles, depth, cycle_parts), class_count, 2 * chips)
    sums = sums.reshape(2 * chips, class_count + 1, depth, cycle_parts)
    shares = lax.all_to_all(sums, "cls", 0, 0, tiled=True)
    class_means = means_of(shares)
    class_means = jnp.transpose(class_means, (1, 0, 2))

    images = [flat, mate, partner, partner_mate]
    places = jnp.stack([(row % 2 ^ chip) * 2 + (core ^ other) for chip in range(2) for other in range(2)])
    best = score(places.astype(jnp.int32), images)
    sent = facing(best)
    mine, others = best[:, :class_count], sent[:, LANES // 2 : LANES // 2 + class_count]
    low = jnp.where(row < chips // 2, mine, others)
    high = jnp.where(row < chips // 2, others, mine)
    best_scores = jnp.concatenate([low, high], axis=0)
    return (best_scores, class_means)


def solution(mesh):
    return jax.shard_map(
        on_device,
        mesh=mesh,
        in_specs=(
            P(None, ("dom", "cls"), None, None),
            P(None, "cls", None),
            P(("dom", "cls"), None),
            P(("dom", "cls")),
            P(("dom", "cls"), None),
            P(("dom", "cls"), None),
        ),
        out_specs=(P("dom", "cls"), P("dom", "cls", None)),
        check_vma=False,
    )
```
